32 devices in a mesh: tm: 8 (over z, x), chan: 4 (over y, core).
Axes of the slice: x: 2, y: 2, z: 4, core: 2. Of those that a mesh axis runs over, the one named last changes fastest.
Arguments:
- record: float32 [8192, 1024], P('tm', 'chan'), may hold values from -120 to 120
- test_matrix: float32 [64, 1024, 128], P(None, 'chan'), may hold values from -0.0234375 to 0.0234375
Outputs:
- basis: float32 [8192, 128], P('tm')
- coeffs: float32 [64, 1024, 128], P('tm', 'chan')
The draws below stay inside these ranges and needn't reach their ends.
All inputs are finite; a program needn't handle non-finite values.
Results may differ from the reference program's by a relative error of at most 0.00024.
Values sent between devices are 32-bit elements; how exact they have to be, the bound alone decides.
No kernel may reach another device: no remote copies, remote signals or barrier semaphores. Data moves between devices by JAX's collectives and lax.ppermute only.
A program may use at most 256 MiB of HBM per device.

```python
import jax
import jax.numpy as jnp
from jax import lax

C = 1024
L = 64
K = 128
NT = 8192


def draw_record(key, part):
    key_base = jax.random.fold_in(key, 11)
    key_chan = jax.random.fold_in(key, 12)
    steps = jnp.arange(NT, dtype=jnp.float32)
    ramp = 1.0 + 2.0 * steps / jnp.float32(max(NT - 1, 1))
    chan_scale = jnp.exp(jax.random.uniform(key_chan, (C,), jnp.float32, 0.0, 2.302585))
    base = jax.random.truncated_normal(key_base, -4.0, 4.0, (NT, C), jnp.float32)
    return (base * ramp[:, None] * chan_scale[None, :]).astype(jnp.float32)


def levels(own_key, extent, shards, least, largest):
    factor_of = 1.0
    for axis_at, blocks in shards:
        steps = jax.random.uniform(jax.random.fold_in(jax.random.fold_in(own_key, 6), axis_at), (blocks,), jnp.float32, least / len(shards), largest / len(shards))
        factor_of = factor_of * jnp.repeat(jnp.exp(steps), extent[axis_at] // blocks).reshape((-1,) + (1,) * (len(extent) - 1 - axis_at))
    return factor_of


def gaussian(stream_key, shape, deviation, bound, shards=(), held_as=jnp.bfloat16):
    entries = deviation * jax.random.normal(stream_key, shape, jnp.float32)
    if shards:
        entries = entries * levels(stream_key, shape, shards, -0.22, 0.18)
    return jnp.clip(entries, -bound, bound).astype(held_as)


def setup_inputs(seed: int = 0) -> dict:
    keys = jax.random.split(jax.random.key(seed), 3)
    record = draw_record(jax.random.fold_in(keys[2], 71), 0)
    test_matrix = gaussian(keys[1], (L, C, K), (C * L) ** -0.5, 0.0234375, ((1, 4),), jnp.float32)
    return dict(record=record, test_matrix=test_matrix)


def reference(record, test_matrix):
    hi = lax.Precision.HIGHEST
    padded = jnp.concatenate([record, jnp.zeros((L - 1, C), jnp.float32)], axis=0)
    sketch = jnp.zeros((NT, K), jnp.float32)
    for lag in range(L):
        sketch = sketch + jnp.dot(padded[lag:lag + NT].astype(jnp.float32), test_matrix[lag].astype(jnp.float32), precision=hi, preferred_element_type=jnp.float32)
    gram = jnp.dot(sketch.T.astype(jnp.float32), sketch.astype(jnp.float32), precision=hi, preferred_element_type=jnp.float32)
    lower = jnp.linalg.cholesky(gram)
    basis = lax.linalg.triangular_solve(lower, sketch, left_side=False, lower=True, transpose_a=True) * jnp.sqrt(jnp.float32(NT))
    scale = 1.0 / jnp.sqrt(jnp.float32(NT))
    coeffs = []
    for lag in range(L):
        coeffs.append(jnp.dot(padded[lag:lag + NT].T.astype(jnp.float32), basis.astype(jnp.float32), precision=hi, preferred_element_type=jnp.float32) * scale)
    return (basis, jnp.stack(coeffs, axis=0))
```

```python
import functools

import jax
import jax.numpy as jnp
from jax import lax
from jax.experimental import pallas as pl
from jax.experimental.pallas import tpu as pltpu
from jax.sharding import PartitionSpec as P


F32 = jnp.float32
BF16 = jnp.bfloat16
STEP = 16
VMEM_BYTES = 56 * 2**20


def split(x):
    high = x.astype(BF16)
    return high, (x - high.astype(F32)).astype(BF16)


def three(a_high, a_low, b_high, b_low):
    dot = functools.partial(jnp.dot, preferred_element_type=F32)
    return dot(a_high, b_high) + dot(a_high, b_low) + dot(a_low, b_high)


def sketch_kernel(record_ref, weight_ref, out_ref, high, low, even, odd):
    pair = pl.program_id(0)
    rows, width = out_ref.shape
    groups = weight_ref.shape[0]
    tiles = 3
    tile = (rows + STEP) // tiles

    @pl.when(pair == 0)
    def _():
        high[...], low[...] = split(record_ref[...])
        out_ref[...] = jnp.zeros_like(out_ref)

    weight = jnp.concatenate(
        [jnp.concatenate([weight_ref[a, 0], weight_ref[a, 1]], axis=1) for a in range(groups)],
        axis=0,
    )
    weight_high, weight_low = split(weight)
    for first in range(0, tiles * tile, tile):
        starts = [first + a * STEP for a in range(groups)]
        left_high = jnp.concatenate([high[s : s + tile] for s in starts], axis=1)
        left_low = jnp.concatenate([low[s : s + tile] for s in starts], axis=1)
        total = three(left_high, left_low, weight_high, weight_low)
        even[first : first + tile] = total[:, :width]
        odd[first : first + tile] = total[:, width:]
    out_ref[...] += even[pl.ds(2 * pair, rows), :] + odd[pl.ds(2 * pair + 1, rows), :]


def sketch(extended, weights, rows):
    lags, chans, width = weights.shape
    length = extended.shape[0]
    return pl.pallas_call(
        sketch_kernel,
        grid=(STEP // 2,),
        in_specs=[
            pl.BlockSpec((length, chans), lambda i: (0, 0)),
            pl.BlockSpec((lags // STEP, 2, chans, width), lambda i: (0, i, 0, 0)),
        ],
        out_specs=pl.BlockSpec((rows, width), lambda i: (0, 0)),
        out_shape=jax.ShapeDtypeStruct((rows, width), F32),
        scratch_shapes=[
            pltpu.VMEM((length, chans), BF16),
            pltpu.VMEM((length, chans), BF16),
            pltpu.VMEM((rows + STEP, width), F32),
            pltpu.VMEM((rows + STEP, width), F32),
        ],
        compiler_params=pltpu.CompilerParams(vmem_limit_bytes=VMEM_BYTES),
        cost_estimate=pl.CostEstimate(
            flops=6 * rows * lags * chans * width,
            bytes_accessed=4 * (lags * chans * width + length * chans + rows * width),
            transcendentals=0,
        ),
        name="sketch",
    )(extended, weights.reshape(lags // STEP, STEP, chans, width))


def turn_kernel(block_ref, high_ref, low_ref):
    high_ref[...], low_ref[...] = split(block_ref[...].T)


def turn(block):
    rows, chans = block.shape
    return pl.pallas_call(
        turn_kernel,
        out_shape=(jax.ShapeDtypeStruct((chans, rows), BF16),) * 2,
        compiler_params=pltpu.CompilerParams(vmem_limit_bytes=VMEM_BYTES),
        cost_estimate=pl.CostEstimate(
            flops=0, bytes_accessed=8 * rows * chans, transcendentals=0
        ),
        name="turn",
    )(block)


def lagged_kernel(blocks, lag_ref, *refs):
    highs, lows, (sketch_ref, out_ref) = refs[:blocks], refs[blocks : 2 * blocks], refs[2 * blocks :]
    rows = highs[0].shape[1]
    width = out_ref.shape[2]
    rim = sketch_ref.shape[1] - rows
    start = rim - (lag_ref[0] + 2 * pl.program_id(0))
    total = jnp.zeros((out_ref.shape[1], 2 * width), F32)
    for b in range(blocks):
        moved = jnp.concatenate(
            [sketch_ref[b, pl.ds(start, rows), :], sketch_ref[b, pl.ds(start - 1, rows), :]], axis=1
        )
        moved_high, moved_low = split(moved)
        total = total + three(highs[b][...], lows[b][...], moved_high, moved_low)
    out_ref[0] = total[:, :width]
    out_ref[1] = total[:, width:]


def lagged(lag, turned, sketches, lags):
    blocks, length, width = sketches.shape
    chans, rows = turned[0][0].shape
    whole = pl.BlockSpec((chans, rows), lambda i: (0, 0))
    return pl.pallas_call(
        functools.partial(lagged_kernel, blocks),
        grid=(lags // 2,),
        in_specs=[pl.BlockSpec(memory_space=pltpu.SMEM)]
        + [whole] * (2 * blocks)
        + [pl.BlockSpec(sketches.shape, lambda i: (0, 0, 0))],
        out_specs=pl.BlockSpec((2, chans, width), lambda i: (i, 0, 0)),
        out_shape=jax.ShapeDtypeStruct((lags, chans, width), F32),
        compiler_params=pltpu.CompilerParams(vmem_limit_bytes=VMEM_BYTES),
        cost_estimate=pl.CostEstimate(
            flops=6 * blocks * rows * chans * lags * width,
            bytes_accessed=4 * (blocks * rows * chans + lags * chans * width + blocks * length * width),
            transcendentals=0,
        ),
        name="lagged",
    )(lag.reshape(1), *[h for h, _ in turned], *[l for _, l in turned], sketches)


def on_device(record, test_matrix):
    rows, chans = record.shape
    lags, _, width = test_matrix.shape
    n_time = lax.axis_size("tm")
    n_chan = lax.axis_size("chan")
    here = lax.axis_index("tm")
    mine = lax.axis_index("chan")
    half = n_time // 2
    mids = n_time // 4
    per = lags // n_time
    rim = lags

    def to(block, target, axis="tm"):
        count = lax.axis_size(axis)
        return lax.ppermute(block, axis, [(i, target(i)) for i in range(count) if 0 <= target(i) < count])

    def beside(block):
        return to(block, lambda i: i ^ 1)

    def across(block):
        return to(block, lambda i: (i + half) % n_time)

    before = to(record[rows - rim :], lambda i: i + 1)
    after = to(record[:rim], lambda i: i - 1)
    record_across = [across(record[s : s + rows // 2]) for s in (0, rows // 2)]
    record_beside = beside(record)
    record_both = [beside(r) for r in record_across]

    extended = jnp.concatenate([before, record, after], axis=0)
    partial_value = sketch(extended, test_matrix, rows + rim)
    share = (rows + rim) // n_chan

    def share_of(owner):
        return lax.dynamic_slice_in_dim(partial_value, owner * share, share, 0)

    own = share_of(mine)
    for s in range(1, n_chan):
        own = own + to(share_of((mine + s) % n_chan), lambda i: (i + s) % n_chan, "chan")
    row = mine * share + lax.broadcasted_iota(jnp.int32, (share, 1), 0)
    own = jnp.where((row >= rim) | (here > 0), own, 0.0)

    shares = jnp.stack([own, beside(own), across(own), to(own, lambda i: ((i ^ 1) + half) % n_time)])
    blocks = shares.shape[0]
    sketches = jnp.zeros((blocks, n_chan * share, width), F32)
    sketches = lax.dynamic_update_slice(sketches, shares, (0, mine * share, 0))
    for s in range(1, n_chan):
        got = to(shares, lambda i: (i + s) % n_chan, "chan")
        sketches = lax.dynamic_update_slice(sketches, got, (0, ((mine + n_chan - s) % n_chan) * share, 0))

    kept = jnp.where(row[None] >= rim, shares, 0.0).reshape(blocks * share, width)
    gram = lax.dot_general(
        kept, kept, (((0,), (0,)), ((), ())), precision=lax.Precision.HIGHEST, preferred_element_type=F32
    )
    distance = 1
    while distance < n_chan:
        gram = gram + to(gram, lambda i: i ^ distance, "chan")
        distance *= 2
    distance = 2
    while distance < half:
        gram = gram + to(gram, lambda i: i ^ distance)
        distance *= 2
    lower = jnp.linalg.cholesky(gram)
    inverse = lax.linalg.triangular_solve(
        lower, jnp.eye(width, dtype=F32), left_side=True, lower=True
    )

    turned = [turn(record), turn(record_beside)]
    turned.append(turn(jnp.concatenate(record_across, axis=0)))
    turned.append(turn(jnp.concatenate(record_both, axis=0)))

    middle = (here % half) // 2
    outer = here - 2 * middle

    def part(step):
        owner = outer + 2 * ((middle + step) % mids)
        return lagged(owner * per, turned, sketches, per)

    received = []
    for s in range(1, mids):
        route = lambda i: i - 2 * ((i % half) // 2) + 2 * (((i % half) // 2 + s) % mids)
        received.append(to(part(s), route))
    total = part(0)
    for r in received:
        total = total + r

    def whitened(x):
        return lax.dot_general(
            x, inverse, (((x.ndim - 1,), (1,)), ((), ())),
            precision=lax.Precision.HIGHEST, preferred_element_type=F32,
        )

    basis = whitened(sketches[0, rim:]) * jnp.sqrt(F32(rows * n_time))
    return basis, whitened(total)


def solution(mesh):
    return jax.shard_map(
        on_device,
        mesh=mesh,
        in_specs=(P("tm", "chan"), P(None, "chan", None)),
        out_specs=(P("tm", None), P("tm", "chan", None)),
        check_vma=False,
    )
```

```python
import functools

import jax
import jax.numpy as jnp
from jax import lax
from jax.experimental import pallas as pl
from jax.experimental.pallas import tpu as pltpu
from jax.sharding import PartitionSpec as P


F32 = jnp.float32
BF16 = jnp.bfloat16
HIGHEST = lax.Precision.HIGHEST
STEP = 16
SMEM = pl.BlockSpec(memory_space=pltpu.SMEM)
VMEM = pl.BlockSpec(memory_space=pltpu.VMEM)


def cost(flops, size):
    return pl.CostEstimate(flops=flops, bytes_accessed=size, transcendentals=0)


def split(x):
    high = x.astype(BF16)
    return high, (x - high.astype(F32)).astype(BF16)


def three(a_high, a_low, b_high, b_low):
    dot = functools.partial(jnp.dot, preferred_element_type=F32)
    return dot(a_high, b_high) + dot(a_high, b_low) + dot(a_low, b_high)


def sketch_kernel(owner_ref, before_ref, record_ref, after_ref, weight_ref, *refs):
    *outs, high, low, even, odd, total = refs
    pair = pl.program_id(0)
    rows, width = total.shape
    groups = weight_ref.shape[0]
    tiles = 3
    tile = (rows + STEP) // tiles

    @pl.when(pair == 0)
    def _():
        first = 0
        for ref in (before_ref, record_ref, after_ref):
            size = ref.shape[0]
            high[first : first + size], low[first : first + size] = split(ref[...])
            first += size
        total[...] = jnp.zeros_like(total)

    weight = jnp.concatenate(
        [jnp.concatenate([weight_ref[a, 0], weight_ref[a, 1]], axis=1) for a in range(groups)],
        axis=0,
    )
    weight_high, weight_low = split(weight)
    for first in range(0, tiles * tile, tile):
        starts = [first + a * STEP for a in range(groups)]
        left_high = jnp.concatenate([high[s : s + tile] for s in starts], axis=1)
        left_low = jnp.concatenate([low[s : s + tile] for s in starts], axis=1)
        value = three(left_high, left_low, weight_high, weight_low)
        even[first : first + tile] = value[:, :width]
        odd[first : first + tile] = value[:, width:]
    total[...] += even[pl.ds(2 * pair, rows), :] + odd[pl.ds(2 * pair + 1, rows), :]

    @pl.when(pair == pl.num_programs(0) - 1)
    def _():
        share = rows // len(outs)
        for s, out in enumerate(outs):
            owner = lax.rem(owner_ref[0] + s, len(outs))
            out[...] = total[pl.ds(pl.multiple_of(owner * share, 8), share), :]


def sketch(owner, before, record, after, weights, shares):
    lags, chans, width = weights.shape
    rows = before.shape[0] + record.shape[0]
    length = rows + after.shape[0]
    share = rows // shares
    return pl.pallas_call(
        sketch_kernel,
        grid=(STEP // 2,),
        in_specs=[SMEM, VMEM, VMEM, VMEM]
        + [pl.BlockSpec((lags // STEP, 2, chans, width), lambda i: (0, i, 0, 0))],
        out_specs=[VMEM] * shares,
        out_shape=[jax.ShapeDtypeStruct((share, width), F32)] * shares,
        scratch_shapes=[
            pltpu.VMEM((length, chans), BF16),
            pltpu.VMEM((length, chans), BF16),
            pltpu.VMEM((rows + STEP, width), F32),
            pltpu.VMEM((rows + STEP, width), F32),
            pltpu.VMEM((rows, width), F32),
        ],
        compiler_params=pltpu.CompilerParams(vmem_limit_bytes=58 * 2**20),
        cost_estimate=cost(
            6 * rows * lags * chans * width,
            4 * (lags * chans * width + length * chans + rows * width),
        ),
        name="sketch",
    )(owner.reshape(1), before, record, after, weights.reshape(lags // STEP, STEP, chans, width))


def turn_kernel(block_ref, high_ref, low_ref):
    high_ref[...], low_ref[...] = split(block_ref[...].T)


def turn(block):
    rows, chans = block.shape
    return pl.pallas_call(
        turn_kernel,
        in_specs=[VMEM],
        out_specs=[VMEM] * 2,
        out_shape=[jax.ShapeDtypeStruct((chans, rows), BF16)] * 2,
        compiler_params=pltpu.CompilerParams(vmem_limit_bytes=12 * 2**20),
        cost_estimate=cost(0, 8 * rows * chans),
        name="turn",
    )(block)


def assemble_kernel(rim, bits_ref, own_ref, got_ref, out_ref, gram_ref):
    pieces, share, width = own_ref.shape
    blocks = pieces // 2
    low, high = bits_ref[0], bits_ref[1]

    def place(first_ref, second_ref):
        for b in range(blocks):
            for q in range(2):
                owner = 2 * jnp.bitwise_xor(high, q)
                first = pl.multiple_of(owner * share, 8)
                out_ref[b, pl.ds(first, share), :] = first_ref[2 * b + q]
                out_ref[b, pl.ds(pl.multiple_of(first + share, 8), share), :] = second_ref[blocks * q + b]

    @pl.when(low == 0)
    def _():
        place(own_ref, got_ref)

    @pl.when(low == 1)
    def _():
        place(got_ref, own_ref)

    gram = jnp.zeros((width, width), F32)
    for b in range(blocks):
        value = out_ref[b, rim:, :]
        gram = gram + lax.dot_general(
            value, value, (((0,), (0,)), ((), ())), precision=HIGHEST, preferred_element_type=F32
        )
    gram_ref[...] = gram


def assemble(bits, own, got, rim, shares):
    pieces, share, width = own.shape
    blocks = pieces // 2
    return pl.pallas_call(
        functools.partial(assemble_kernel, rim),
        in_specs=[SMEM, VMEM, VMEM],
        out_specs=[VMEM] * 2,
        out_shape=[
            jax.ShapeDtypeStruct((blocks, shares * share, width), F32),
            jax.ShapeDtypeStruct((width, width), F32),
        ],
        compiler_params=pltpu.CompilerParams(vmem_limit_bytes=20 * 2**20),
        cost_estimate=cost(
            12 * blocks * shares * share * width * width, 8 * blocks * shares * share * width
        ),
        name="assemble",
    )(bits, own, got)


def factor_kernel(gram_ref, out_ref):
    size = gram_ref.shape[0]
    tile = 8
    groups = size // tile
    row_of = lax.broadcasted_iota(jnp.int32, (tile, size), 0)
    col_of = lax.broadcasted_iota(jnp.int32, (tile, size), 1)
    g = [gram_ref[q * tile : (q + 1) * tile, :] for q in range(groups)]
    x = [jnp.where(col_of == row_of + q * tile, 1.0, 0.0).astype(F32) for q in range(groups)]
    for p in range(groups):
        pivots = jnp.ones((tile, 1), F32)
        for r in range(tile):
            j = p * tile + r
            g_row = g[p][r : r + 1, :]
            x_row = x[p][r : r + 1, :]
            pivot = g_row[:, j : j + 1]
            pivots = jnp.where(row_of[:, :1] == r, pivot, pivots)
            inverse = 1.0 / pivot
            g_row = g_row * inverse
            x_row = x_row * inverse
            for q in range(p, groups):
                column = g[q][:, j : j + 1]
                if q == p:
                    column = jnp.where(row_of[:, :1] > r, column, 0.0)
                g[q] = g[q] - column * g_row
                x[q] = x[q] - column * x_row
        out_ref[p * tile : (p + 1) * tile, :] = x[p] * (1.0 / jnp.sqrt(pivots))


def factor(gram):
    return pl.pallas_call(
        factor_kernel,
        in_specs=[VMEM],
        out_specs=VMEM,
        out_shape=jax.ShapeDtypeStruct(gram.shape, F32),
        compiler_params=pltpu.CompilerParams(vmem_limit_bytes=8 * 2**20),
        cost_estimate=cost(9 * 10**9, 2**17),
        name="factor",
    )(gram)


def lagged_kernel(places, lag_ref, *refs):
    count = len(places)
    highs, lows, (sketch_ref, out_ref) = refs[:count], refs[count : 2 * count], refs[2 * count :]
    width = out_ref.shape[2]
    rim = places[0][2]
    start = rim - (lag_ref[0] + 2 * pl.program_id(0))
    total = jnp.zeros((out_ref.shape[1], 2 * width), F32)
    for (block, first, _), high, low in zip(places, highs, lows):
        rows = high.shape[1]
        moved = jnp.concatenate(
            [
                sketch_ref[block, pl.ds(start + first, rows), :],
                sketch_ref[block, pl.ds(start + first - 1, rows), :],
            ],
            axis=1,
        )
        moved_high, moved_low = split(moved)
        total = total + three(high[...], low[...], moved_high, moved_low)
    out_ref[0] = total[:, :width]
    out_ref[1] = total[:, width:]


def lagged(lag, turned, places, sketches, lags):
    blocks, length, width = sketches.shape
    chans = turned[0][0].shape[0]
    rows = sum(h.shape[1] for h, _ in turned)
    return pl.pallas_call(
        functools.partial(lagged_kernel, places),
        grid=(lags // 2,),
        in_specs=[SMEM] + [VMEM] * (2 * len(turned) + 1),
        out_specs=pl.BlockSpec((2, chans, width), lambda i: (i, 0, 0)),
        out_shape=jax.ShapeDtypeStruct((lags, chans, width), F32),
        compiler_params=pltpu.CompilerParams(vmem_limit_bytes=28 * 2**20),
        cost_estimate=cost(
            6 * rows * chans * lags * width,
            4 * (rows * chans + lags * chans * width + blocks * length * width),
        ),
        name="lagged",
    )(lag.reshape(1), *[h for h, _ in turned], *[l for _, l in turned], sketches)


def finish_kernel(chunks, inverse_ref, kept_ref, *refs):
    *received, out_ref = refs
    lags, chans, width = out_ref.shape
    size = lags // chunks
    inverse_high, inverse_low = split(inverse_ref[...].T)
    for n in range(chunks):
        part = slice(n * size, (n + 1) * size)
        total = kept_ref[part]
        for ref in received[n::chunks]:
            total = total + ref[...]
        high, low = split(total.reshape(size * chans, width))
        out_ref[part] = three(high, low, inverse_high, inverse_low).reshape(size, chans, width)


def finish(inverse, kept, received, chunks):
    lags, chans, width = kept.shape
    return pl.pallas_call(
        functools.partial(finish_kernel, chunks),
        in_specs=[VMEM] * (2 + len(received)),
        out_specs=VMEM,
        out_shape=jax.ShapeDtypeStruct(kept.shape, F32),
        compiler_params=pltpu.CompilerParams(vmem_limit_bytes=28 * 2**20),
        cost_estimate=cost(6 * lags * chans * width * width, 12 * lags * chans * width),
        name="finish",
    )(inverse, kept, *received)


def on_device(record, test_matrix):
    rows, _ = record.shape
    lags, _, _ = test_matrix.shape
    n_time = lax.axis_size("tm")
    n_chan = lax.axis_size("chan")
    here = lax.axis_index("tm")
    mine = lax.axis_index("chan")
    half = n_time // 2
    mids = n_time // 4
    per = lags // n_time
    rim = lags

    def to(block, target, axis="tm"):
        count = lax.axis_size(axis)
        route = [(i, target(i)) for i in range(count) if 0 <= target(i) < count]
        return lax.ppermute(block, axis, route)

    def to_both(block, target):
        route = []
        for t in range(n_time):
            for c in range(n_chan):
                a, b = target(t, c)
                route.append((t * n_chan + c, a * n_chan + b))
        return lax.ppermute(block, ("tm", "chan"), route)

    def beside(t):
        return t ^ 1

    def across(t):
        return (t + half) % n_time

    before = to(record[rows - rim :], lambda i: i + 1)
    after = to(record[:rim], lambda i: i - 1)
    cut = [0, rows // 2, rows]
    parts = [record[a:b] for a, b in zip(cut, cut[1:])]
    beside_record = to(record, beside)
    across_parts = [to(part, across) for part in parts]
    both_parts = [to(part, beside) for part in across_parts]

    shares = sketch(mine, before, record, after, test_matrix, n_chan)
    share = shares[0].shape[0]
    own = shares[0]
    for s in range(1, n_chan):
        own = own + to(shares[s], lambda i: (i + s) % n_chan, "chan")
    row = mine * share + lax.broadcasted_iota(jnp.int32, (share, 1), 0)
    own = jnp.where((row >= rim) | (here > 0), own, 0.0)[None]

    def even(c):
        return c % 2 == 0

    got = to_both(own, lambda t, c: (t, c ^ 2) if even(c) else (across(t), c))
    own = jnp.concatenate([own, got], axis=0)
    got = to_both(own, lambda t, c: (across(t), c) if even(c) else (beside(t), c))
    own = jnp.concatenate([own, got], axis=0)
    got = to_both(own, lambda t, c: (beside(t), c) if even(c) else (t, c ^ 2))
    own = jnp.concatenate([own, got], axis=0)
    got = to(own, lambda i: i ^ 1, "chan")
    sketches, gram = assemble(jnp.stack([mine % 2, mine // 2]), own, got, rim, n_chan)
    distance = 2
    while distance < half:
        gram = gram + to(gram, lambda i: i ^ distance)
        distance *= 2

    turned = [turn(record)]
    turned += [turn(p) for p in across_parts]
    turned += [turn(beside_record)]
    turned += [turn(p) for p in both_parts]
    places = [(0, 0, rim)] + [(1, a, rim) for a in cut[:-1]] + [(2, 0, rim)] + [(3, a, rim) for a in cut[:-1]]

    middle = (here % half) // 2
    outer = here - 2 * middle

    def owner_lag(step):
        return (outer + 2 * ((middle + step) % mids)) * per

    chunks = 2 if per % 4 == 0 else 1
    size = per // chunks
    received = []
    for s in range(1, mids):
        def route(i):
            m = (i % half) // 2
            return i - 2 * m + 2 * ((m + s) % mids)

        for n in range(chunks):
            part = lagged(owner_lag(s) + n * size, turned, places, sketches, size)
            received.append(to(part, route))
    kept = lagged(owner_lag(0), turned, places, sketches, per)
    inverse = factor(gram)

    def whitened(x):
        return lax.dot_general(
            x, inverse, (((x.ndim - 1,), (1,)), ((), ())), precision=HIGHEST, preferred_element_type=F32
        )

    basis = whitened(sketches[0, rim:]) * jnp.sqrt(F32(rows * n_time))
    return basis, finish(inverse, kept, received, chunks)


def solution(mesh):
    return jax.shard_map(
        on_device,
        mesh=mesh,
        in_specs=(P("tm", "chan"), P(None, "chan", None)),
        out_specs=(P("tm", None), P("tm", "chan", None)),
        check_vma=False,
    )
```

```python
import functools

import jax
import jax.numpy as jnp
from jax import lax
from jax.experimental import pallas as pl
from jax.experimental.pallas import tpu as pltpu
from jax.sharding import PartitionSpec as P


F32 = jnp.float32
BF16 = jnp.bfloat16
HIGHEST = lax.Precision.HIGHEST
STEP = 16
SMEM = pl.BlockSpec(memory_space=pltpu.SMEM)
VMEM = pl.BlockSpec(memory_space=pltpu.VMEM)


def cost(flops, size):
    return pl.CostEstimate(flops=flops, bytes_accessed=size, transcendentals=0)


def split(x):
    high = x.astype(BF16)
    return high, (x - high.astype(F32)).astype(BF16)


def three(a_high, a_low, b_high, b_low):
    dot = functools.partial(jnp.dot, preferred_element_type=F32)
    return dot(a_high, b_high) + dot(a_high, b_low) + dot(a_low, b_high)


def sketch_kernel(owner_ref, before_ref, record_ref, after_ref, weight_ref, *refs):
    keep_ref, give_ref, high, low, even, odd, total = refs
    pair = pl.program_id(0)
    rows, width = total.shape
    groups = weight_ref.shape[0]
    tiles = 3
    tile = (rows + STEP) // tiles

    @pl.when(pair == 0)
    def _():
        first = 0
        for ref in (before_ref, record_ref, after_ref):
            size = ref.shape[0]
            high[first : first + size], low[first : first + size] = split(ref[...])
            first += size
        total[...] = jnp.zeros_like(total)

    weight = jnp.concatenate(
        [jnp.concatenate([weight_ref[a, 0], weight_ref[a, 1]], axis=1) for a in range(groups)],
        axis=0,
    )
    weight_high, weight_low = split(weight)
    for first in range(0, tiles * tile, tile):
        starts = [first + a * STEP for a in range(groups)]
        left_high = jnp.concatenate([high[s : s + tile] for s in starts], axis=1)
        left_low = jnp.concatenate([low[s : s + tile] for s in starts], axis=1)
        value = three(left_high, left_low, weight_high, weight_low)
        even[first : first + tile] = value[:, :width]
        odd[first : first + tile] = value[:, width:]
    total[...] += even[pl.ds(2 * pair, rows), :] + odd[pl.ds(2 * pair + 1, rows), :]

    @pl.when(pair == pl.num_programs(0) - 1)
    def _():
        share = keep_ref.shape[1]
        for ref, flip in ((keep_ref, 0), (give_ref, 1)):
            for n in range(2):
                owner = jnp.bitwise_xor(owner_ref[0], 2 * n + flip)
                ref[n] = total[pl.ds(pl.multiple_of(owner * share, 8), share), :]


def sketch(owner, before, record, after, weights, shares):
    lags, chans, width = weights.shape
    rows = before.shape[0] + record.shape[0]
    length = rows + after.shape[0]
    share = rows // shares
    return pl.pallas_call(
        sketch_kernel,
        grid=(STEP // 2,),
        in_specs=[SMEM, VMEM, VMEM, VMEM]
        + [pl.BlockSpec((lags // STEP, 2, chans, width), lambda i: (0, i, 0, 0))],
        out_specs=[VMEM] * 2,
        out_shape=[jax.ShapeDtypeStruct((2, share, width), F32)] * 2,
        scratch_shapes=[
            pltpu.VMEM((length, chans), BF16),
            pltpu.VMEM((length, chans), BF16),
            pltpu.VMEM((rows + STEP, width), F32),
            pltpu.VMEM((rows + STEP, width), F32),
            pltpu.VMEM((rows, width), F32),
        ],
        compiler_params=pltpu.CompilerParams(vmem_limit_bytes=58 * 2**20),
        cost_estimate=cost(
            6 * rows * lags * chans * width,
            4 * (lags * chans * width + length * chans + rows * width),
        ),
        name="sketch",
    )(owner.reshape(1), before, record, after, weights.reshape(lags // STEP, STEP, chans, width))


def turn_kernel(block_ref, high_ref, low_ref):
    high_ref[...], low_ref[...] = split(block_ref[...].T)


def turn(block):
    rows, chans = block.shape
    return pl.pallas_call(
        turn_kernel,
        in_specs=[VMEM],
        out_specs=[VMEM] * 2,
        out_shape=[jax.ShapeDtypeStruct((chans, rows), BF16)] * 2,
        compiler_params=pltpu.CompilerParams(vmem_limit_bytes=12 * 2**20),
        cost_estimate=cost(0, 8 * rows * chans),
        name="turn",
    )(block)


def assemble_kernel(bits_ref, own_ref, got_ref, out_ref):
    pieces, share, _ = own_ref.shape
    blocks = pieces // 2
    low, high = bits_ref[0], bits_ref[1]

    def place(first_ref, second_ref):
        for b in range(blocks):
            for q in range(2):
                owner = 2 * jnp.bitwise_xor(high, q)
                first = pl.multiple_of(owner * share, 8)
                out_ref[b, pl.ds(first, share), :] = first_ref[2 * b + q]
                out_ref[b, pl.ds(pl.multiple_of(first + share, 8), share), :] = second_ref[blocks * q + b]

    @pl.when(low == 0)
    def _():
        place(own_ref, got_ref)

    @pl.when(low == 1)
    def _():
        place(got_ref, own_ref)


def assemble(bits, own, got, shares):
    pieces, share, width = own.shape
    blocks = pieces // 2
    return pl.pallas_call(
        assemble_kernel,
        in_specs=[SMEM, VMEM, VMEM],
        out_specs=VMEM,
        out_shape=jax.ShapeDtypeStruct((blocks, shares * share, width), F32),
        compiler_params=pltpu.CompilerParams(vmem_limit_bytes=20 * 2**20),
        cost_estimate=cost(0, 8 * blocks * shares * share * width),
        name="assemble",
    )(bits, own, got)


def gram_kernel(rim, bits_ref, own_ref, out_ref):
    pieces, share, width = own_ref.shape
    blocks = pieces // 2
    low, high = bits_ref[0], bits_ref[1]
    kept = lax.broadcasted_iota(jnp.int32, (share, width), 0) >= rim

    def gram(value):
        return lax.dot_general(
            value, value, (((0,), (0,)), ((), ())), precision=HIGHEST, preferred_element_type=F32
        )

    @pl.when(low == 0)
    def _():
        halves = []
        for q in range(2):
            value = jnp.concatenate(
                [jnp.where(kept | (high != q), own_ref[2 * b + q], 0.0) for b in range(blocks)], axis=0
            )
            halves.append(gram(value))
        out_ref[...] = halves[0] + halves[1]

    @pl.when(low == 1)
    def _():
        halves = []
        for q in range(2):
            value = jnp.concatenate([own_ref[blocks * q + b] for b in range(blocks)], axis=0)
            halves.append(gram(value))
        out_ref[...] = halves[0] + halves[1]


def gram_of(bits, own, rim):
    pieces, share, width = own.shape
    return pl.pallas_call(
        functools.partial(gram_kernel, rim),
        in_specs=[SMEM, VMEM],
        out_specs=VMEM,
        out_shape=jax.ShapeDtypeStruct((width, width), F32),
        compiler_params=pltpu.CompilerParams(vmem_limit_bytes=20 * 2**20),
        cost_estimate=cost(12 * pieces * share * width * width, 4 * pieces * share * width),
        name="gram",
    )(bits, own)


def factor_kernel(gram_ref, out_ref):
    size = gram_ref.shape[0]
    tile = 8
    groups = size // tile
    row_of = lax.broadcasted_iota(jnp.int32, (tile, size), 0)
    col_of = lax.broadcasted_iota(jnp.int32, (tile, size), 1)
    g = [gram_ref[q * tile : (q + 1) * tile, :] for q in range(groups)]
    x = [jnp.where(col_of == row_of + q * tile, 1.0, 0.0).astype(F32) for q in range(groups)]
    for p in range(groups):
        pivots = jnp.ones((tile, 1), F32)
        for r in range(tile):
            j = p * tile + r
            g_row = g[p][r : r + 1, :]
            x_row = x[p][r : r + 1, :]
            pivot = g_row[:, j : j + 1]
            pivots = jnp.where(row_of[:, :1] == r, pivot, pivots)
            inverse = 1.0 / pivot
            g_row = g_row * inverse
            x_row = x_row * inverse
            for q in range(p, groups):
                column = g[q][:, j : j + 1]
                if q == p:
                    column = jnp.where(row_of[:, :1] > r, column, 0.0)
                g[q] = g[q] - column * g_row
                x[q] = x[q] - column * x_row
        out_ref[p * tile : (p + 1) * tile, :] = x[p] * (1.0 / jnp.sqrt(pivots))


def factor(gram):
    return pl.pallas_call(
        factor_kernel,
        in_specs=[VMEM],
        out_specs=VMEM,
        out_shape=jax.ShapeDtypeStruct(gram.shape, F32),
        compiler_params=pltpu.CompilerParams(vmem_limit_bytes=8 * 2**20),
        cost_estimate=cost(9 * 10**9, 2**17),
        name="factor",
    )(gram)


def lagged_kernel(places, lag_ref, *refs):
    count = len(places)
    highs, lows, (sketch_ref, out_ref) = refs[:count], refs[count : 2 * count], refs[2 * count :]
    width = out_ref.shape[2]
    rim = places[0][2]
    start = rim - (lag_ref[0] + 2 * pl.program_id(0))
    total = jnp.zeros((out_ref.shape[1], 2 * width), F32)
    for (block, first, _), high, low in zip(places, highs, lows):
        rows = high.shape[1]
        moved = jnp.concatenate(
            [
                sketch_ref[block, pl.ds(start + first, rows), :],
                sketch_ref[block, pl.ds(start + first - 1, rows), :],
            ],
            axis=1,
        )
        moved_high, moved_low = split(moved)
        total = total + three(high[...], low[...], moved_high, moved_low)
    out_ref[0] = total[:, :width]
    out_ref[1] = total[:, width:]


def lagged(lag, turned, places, sketches, lags):
    blocks, length, width = sketches.shape
    chans = turned[0][0].shape[0]
    rows = sum(h.shape[1] for h, _ in turned)
    return pl.pallas_call(
        functools.partial(lagged_kernel, places),
        grid=(lags // 2,),
        in_specs=[SMEM] + [VMEM] * (2 * len(turned) + 1),
        out_specs=pl.BlockSpec((2, chans, width), lambda i: (i, 0, 0)),
        out_shape=jax.ShapeDtypeStruct((lags, chans, width), F32),
        compiler_params=pltpu.CompilerParams(vmem_limit_bytes=20 * 2**20),
        cost_estimate=cost(
            6 * rows * chans * lags * width,
            4 * (rows * chans + lags * chans * width + blocks * length * width),
        ),
        name="lagged",
    )(lag.reshape(1), *[h for h, _ in turned], *[l for _, l in turned], sketches)


def finish_kernel(chunks, inverse_ref, kept_ref, *refs):
    *received, out_ref = refs
    lags, chans, width = out_ref.shape
    size = lags // chunks
    inverse_high, inverse_low = split(inverse_ref[...].T)
    for n in range(chunks):
        part = slice(n * size, (n + 1) * size)
        total = kept_ref[part]
        for ref in received[n::chunks]:
            total = total + ref[...]
        high, low = split(total.reshape(size * chans, width))
        out_ref[part] = three(high, low, inverse_high, inverse_low).reshape(size, chans, width)


def finish(inverse, kept, received, chunks):
    lags, chans, width = kept.shape
    return pl.pallas_call(
        functools.partial(finish_kernel, chunks),
        in_specs=[VMEM] * (2 + len(received)),
        out_specs=VMEM,
        out_shape=jax.ShapeDtypeStruct(kept.shape, F32),
        compiler_params=pltpu.CompilerParams(vmem_limit_bytes=20 * 2**20),
        cost_estimate=cost(6 * lags * chans * width * width, 12 * lags * chans * width),
        name="finish",
    )(inverse, kept, *received)


def on_device(record, test_matrix):
    rows, _ = record.shape
    lags, _, _ = test_matrix.shape
    n_time = lax.axis_size("tm")
    n_chan = lax.axis_size("chan")
    here = lax.axis_index("tm")
    mine = lax.axis_index("chan")
    half = n_time // 2
    mids = n_time // 4
    per = lags // n_time
    rim = lags

    def to(block, target, axis="tm"):
        count = lax.axis_size(axis)
        route = [(i, target(i)) for i in range(count) if 0 <= target(i) < count]
        return lax.ppermute(block, axis, route)

    def to_both(block, target):
        route = []
        for t in range(n_time):
            for c in range(n_chan):
                a, b = target(t, c)
                route.append((t * n_chan + c, a * n_chan + b))
        return lax.ppermute(block, ("tm", "chan"), route)

    def beside(t):
        return t ^ 1

    def across(t):
        return (t + half) % n_time

    before = to(record[rows - rim :], lambda i: i + 1)
    after = to(record[:rim], lambda i: i - 1)
    cut = [0, rows // 2, 3 * rows // 4, rows]
    parts = [record[a:b] for a, b in zip(cut, cut[1:])]
    beside_record = to(record, beside)
    across_parts = [to(part, across) for part in parts]
    both_parts = [to(part, beside) for part in across_parts]

    keep, give = sketch(mine, before, record, after, test_matrix, n_chan)
    share = keep.shape[1]
    keep = keep + to(give, lambda i: i ^ 1, "chan")
    own = keep[:1] + to(keep[1:], lambda i: i ^ 2, "chan")
    row = mine * share + lax.broadcasted_iota(jnp.int32, (1, share, 1), 1)
    own = jnp.where((row >= rim) | (here > 0), own, 0.0)

    def even(c):
        return c % 2 == 0

    got = to_both(own, lambda t, c: (t, c ^ 2) if even(c) else (across(t), c))
    own = jnp.concatenate([own, got], axis=0)
    got = to_both(own, lambda t, c: (across(t), c) if even(c) else (beside(t), c))
    own = jnp.concatenate([own, got], axis=0)
    got = to_both(own, lambda t, c: (beside(t), c) if even(c) else (t, c ^ 2))
    own = jnp.concatenate([own, got], axis=0)
    got = to(own, lambda i: i ^ 1, "chan")
    bits = jnp.stack([mine % 2, mine // 2])
    gram = gram_of(bits, own, rim)
    distance = 2
    while distance < half:
        gram = gram + to(gram, lambda i: i ^ distance)
        distance *= 2
    gram = gram + to(gram, lambda i: i ^ 1, "chan")
    sketches = assemble(bits, own, got, n_chan)

    turned = [turn(record)]
    turned += [turn(p) for p in across_parts]
    turned += [turn(beside_record)]
    turned += [turn(p) for p in both_parts]
    places = [(0, 0, rim)] + [(1, a, rim) for a in cut[:-1]] + [(2, 0, rim)] + [(3, a, rim) for a in cut[:-1]]

    middle = (here % half) // 2
    outer = here - 2 * middle

    def owner_lag(step):
        return (outer + 2 * ((middle + step) % mids)) * per

    chunks = 2 if per % 4 == 0 else 1
    size = per // chunks
    received = []
    for s in range(1, mids):
        def route(i):
            m = (i % half) // 2
            return i - 2 * m + 2 * ((m + s) % mids)

        for n in range(chunks):
            part = lagged(owner_lag(s) + n * size, turned, places, sketches, size)
            received.append(to(part, route))
    kept = lagged(owner_lag(0), turned, places, sketches, per)
    inverse = factor(gram)

    def whitened(x):
        return lax.dot_general(
            x, inverse, (((x.ndim - 1,), (1,)), ((), ())), precision=HIGHEST, preferred_element_type=F32
        )

    basis = whitened(sketches[0, rim:]) * jnp.sqrt(F32(rows * n_time))
    return basis, finish(inverse, kept, received, chunks)


def solution(mesh):
    return jax.shard_map(
        on_device,
        mesh=mesh,
        in_specs=(P("tm", "chan"), P(None, "chan", None)),
        out_specs=(P("tm", None), P("tm", "chan", None)),
        check_vma=False,
    )
```

```python
import functools

import jax
import jax.numpy as jnp
from jax import lax
from jax.experimental import pallas as pl
from jax.experimental.pallas import tpu as pltpu
from jax.sharding import PartitionSpec as P


F32 = jnp.float32
BF16 = jnp.bfloat16
HIGHEST = lax.Precision.HIGHEST
STEP = 16
SMEM = pl.BlockSpec(memory_space=pltpu.SMEM)
VMEM = pl.BlockSpec(memory_space=pltpu.VMEM)


def cost(flops, size):
    return pl.CostEstimate(flops=flops, bytes_accessed=size, transcendentals=0)


def split(x):
    high = x.astype(BF16)
    return high, (x - high.astype(F32)).astype(BF16)


def three(a_high, a_low, b_high, b_low):
    dot = functools.partial(jnp.dot, preferred_element_type=F32)
    return dot(a_high, b_high) + dot(a_high, b_low) + dot(a_low, b_high)


def sketch_kernel(place_ref, before_ref, record_ref, after_ref, weight_ref, *refs):
    keep_ref, give_ref, high, low, even, odd, total, buffer, arrived = refs
    pair = pl.program_id(0)
    rows, width = total.shape
    groups = weight_ref.shape[0]

    def fetch(n):
        slot = lax.rem(n, 2)
        return pltpu.make_async_copy(weight_ref.at[:, pl.ds(2 * n, 2)], buffer.at[slot], arrived.at[slot])

    @pl.when(pair == 0)
    def _():
        fetch(pair).start()

    @pl.when(pair + 1 < pl.num_programs(0))
    def _():
        fetch(pair + 1).start()

    tiles = 3
    tile = (rows + STEP) // tiles

    @pl.when(pair == 0)
    def _():
        first = 0
        for ref in (before_ref, record_ref, after_ref):
            size = ref.shape[0]
            high[first : first + size], low[first : first + size] = split(ref[...])
            first += size
        total[...] = jnp.zeros_like(total)

    fetch(pair).wait()
    slot = lax.rem(pair, 2)
    weight = jnp.concatenate(
        [jnp.concatenate([buffer[slot, a, 0], buffer[slot, a, 1]], axis=1) for a in range(groups)],
        axis=0,
    )
    weight_high, weight_low = split(weight)
    for first in range(0, tiles * tile, tile):
        starts = [first + a * STEP for a in range(groups)]
        left_high = jnp.concatenate([high[s : s + tile] for s in starts], axis=1)
        left_low = jnp.concatenate([low[s : s + tile] for s in starts], axis=1)
        value = three(left_high, left_low, weight_high, weight_low)
        even[first : first + tile] = value[:, :width]
        odd[first : first + tile] = value[:, width:]
    total[...] += even[pl.ds(2 * pair, rows), :] + odd[pl.ds(2 * pair + 1, rows), :]

    @pl.when(pair == pl.num_programs(0) - 1)
    def _():
        share = keep_ref.shape[1]
        for ref, flip in ((keep_ref, 0), (give_ref, 1)):
            for n in range(2):
                owner = jnp.bitwise_xor(place_ref[0], 2 * n + flip)
                ref[n] = total[pl.ds(pl.multiple_of(owner * share, 8), share), :]


def sketch(place, before, record, after, weights, shares):
    lags, chans, width = weights.shape
    rows = before.shape[0] + record.shape[0]
    length = rows + after.shape[0]
    share = rows // shares
    return pl.pallas_call(
        sketch_kernel,
        grid=(STEP // 2,),
        in_specs=[SMEM, VMEM, VMEM, VMEM, pl.BlockSpec(memory_space=pltpu.HBM)],
        out_specs=[VMEM] * 2,
        out_shape=[jax.ShapeDtypeStruct((2, share, width), F32)] * 2,
        scratch_shapes=[
            pltpu.VMEM((length, chans), BF16),
            pltpu.VMEM((length, chans), BF16),
            pltpu.VMEM((rows + STEP, width), F32),
            pltpu.VMEM((rows + STEP, width), F32),
            pltpu.VMEM((rows, width), F32),
            pltpu.VMEM((2, lags // STEP, 2, chans, width), F32),
            pltpu.SemaphoreType.DMA((2,)),
        ],
        compiler_params=pltpu.CompilerParams(vmem_limit_bytes=24 * 2**20),
        cost_estimate=cost(
            6 * rows * lags * chans * width,
            4 * (lags * chans * width + length * chans + rows * width),
        ),
        name="sketch",
    )(place, before, record, after, weights.reshape(lags // STEP, STEP, chans, width))


def turn_kernel(block_ref, high_ref, low_ref):
    high_ref[...], low_ref[...] = split(block_ref[...].T)


def turn(block):
    rows, chans = block.shape
    return pl.pallas_call(
        turn_kernel,
        in_specs=[VMEM],
        out_specs=[VMEM] * 2,
        out_shape=[jax.ShapeDtypeStruct((chans, rows), BF16)] * 2,
        compiler_params=pltpu.CompilerParams(vmem_limit_bytes=12 * 2**20),
        cost_estimate=cost(0, 8 * rows * chans),
        name="turn",
    )(block)


def assemble_kernel(place_ref, own_ref, got_ref, out_ref):
    pieces, share, _ = own_ref.shape
    blocks = pieces // 2
    low, high = place_ref[2], place_ref[3]

    def place(first_ref, second_ref):
        for b in range(blocks):
            for q in range(2):
                owner = 2 * jnp.bitwise_xor(high, q)
                first = pl.multiple_of(owner * share, 8)
                out_ref[b, pl.ds(first, share), :] = first_ref[2 * b + q]
                out_ref[b, pl.ds(pl.multiple_of(first + share, 8), share), :] = second_ref[blocks * q + b]

    @pl.when(low == 0)
    def _():
        place(own_ref, got_ref)

    @pl.when(low == 1)
    def _():
        place(got_ref, own_ref)


def assemble(place, own, got, shares):
    pieces, share, width = own.shape
    blocks = pieces // 2
    return pl.pallas_call(
        assemble_kernel,
        in_specs=[SMEM, VMEM, VMEM],
        out_specs=VMEM,
        out_shape=jax.ShapeDtypeStruct((blocks, shares * share, width), F32),
        compiler_params=pltpu.CompilerParams(vmem_limit_bytes=20 * 2**20),
        cost_estimate=cost(0, 8 * blocks * shares * share * width),
        name="assemble",
    )(place, own, got)


def gram_kernel(rim, place_ref, own_ref, out_ref):
    pieces, share, width = own_ref.shape
    blocks = pieces // 2
    low, high = place_ref[2], place_ref[3]
    kept = lax.broadcasted_iota(jnp.int32, (share, width), 0) >= rim

    def gram(value):
        return lax.dot_general(
            value, value, (((0,), (0,)), ((), ())), precision=HIGHEST, preferred_element_type=F32
        )

    @pl.when(low == 0)
    def _():
        halves = []
        for q in range(2):
            value = jnp.concatenate(
                [jnp.where(kept | (high != q), own_ref[2 * b + q], 0.0) for b in range(blocks)], axis=0
            )
            halves.append(gram(value))
        out_ref[...] = halves[0] + halves[1]

    @pl.when(low == 1)
    def _():
        halves = []
        for q in range(2):
            value = jnp.concatenate([own_ref[blocks * q + b] for b in range(blocks)], axis=0)
            halves.append(gram(value))
        out_ref[...] = halves[0] + halves[1]


def gram_of(place, own, rim):
    pieces, share, width = own.shape
    return pl.pallas_call(
        functools.partial(gram_kernel, rim),
        in_specs=[SMEM, VMEM],
        out_specs=VMEM,
        out_shape=jax.ShapeDtypeStruct((width, width), F32),
        compiler_params=pltpu.CompilerParams(vmem_limit_bytes=20 * 2**20),
        cost_estimate=cost(12 * pieces * share * width * width, 4 * pieces * share * width),
        name="gram",
    )(place, own)


def factor_kernel(gram_ref, other_ref, out_ref):
    size = gram_ref.shape[0]
    tile = 8
    groups = size // tile
    row_of = lax.broadcasted_iota(jnp.int32, (tile, size), 0)
    col_of = lax.broadcasted_iota(jnp.int32, (tile, size), 1)
    tiles = [slice(q * tile, (q + 1) * tile) for q in range(groups)]
    g = [gram_ref[t, :] + other_ref[t, :] for t in tiles]
    x = [jnp.where(col_of == row_of + q * tile, 1.0, 0.0).astype(F32) for q in range(groups)]
    for p in range(groups):
        pivots = jnp.ones((tile, 1), F32)
        for r in range(tile):
            j = p * tile + r
            g_row = g[p][r : r + 1, :]
            x_row = x[p][r : r + 1, :]
            pivot = g_row[:, j : j + 1]
            pivots = jnp.where(row_of[:, :1] == r, pivot, pivots)
            inverse = 1.0 / pivot
            g_row = g_row * inverse
            x_row = x_row * inverse
            for q in range(p, groups):
                column = g[q][:, j : j + 1]
                if q == p:
                    column = jnp.where(row_of[:, :1] > r, column, 0.0)
                g[q] = g[q] - column * g_row
                x[q] = x[q] - column * x_row
        out_ref[p * tile : (p + 1) * tile, :] = x[p] * (1.0 / jnp.sqrt(pivots))


def factor(gram, other):
    return pl.pallas_call(
        factor_kernel,
        in_specs=[VMEM] * 2,
        out_specs=VMEM,
        out_shape=jax.ShapeDtypeStruct(gram.shape, F32),
        compiler_params=pltpu.CompilerParams(vmem_limit_bytes=8 * 2**20),
        cost_estimate=cost(9 * 10**9, 2**17),
        name="factor",
    )(gram, other)


def lagged_kernel(places, lag_ref, *refs):
    count = len(places)
    highs, lows, (sketch_ref, out_ref) = refs[:count], refs[count : 2 * count], refs[2 * count :]
    width = out_ref.shape[2]
    rim = places[0][2]
    start = rim - (lag_ref[0] + 2 * pl.program_id(0))
    total = jnp.zeros((out_ref.shape[1], 2 * width), F32)
    for (block, first, _), high, low in zip(places, highs, lows):
        rows = high.shape[1]
        moved = jnp.concatenate(
            [
                sketch_ref[block, pl.ds(start + first, rows), :],
                sketch_ref[block, pl.ds(start + first - 1, rows), :],
            ],
            axis=1,
        )
        moved_high, moved_low = split(moved)
        total = total + three(high[...], low[...], moved_high, moved_low)
    out_ref[0] = total[:, :width]
    out_ref[1] = total[:, width:]


def lagged(lag, turned, places, sketches, lags):
    blocks, length, width = sketches.shape
    chans = turned[0][0].shape[0]
    rows = sum(h.shape[1] for h, _ in turned)
    return pl.pallas_call(
        functools.partial(lagged_kernel, places),
        grid=(lags // 2,),
        in_specs=[SMEM] + [VMEM] * (2 * len(turned) + 1),
        out_specs=pl.BlockSpec((2, chans, width), lambda i: (i, 0, 0)),
        out_shape=jax.ShapeDtypeStruct((lags, chans, width), F32),
        compiler_params=pltpu.CompilerParams(vmem_limit_bytes=20 * 2**20),
        cost_estimate=cost(
            6 * rows * chans * lags * width,
            4 * (rows * chans + lags * chans * width + blocks * length * width),
        ),
        name="lagged",
    )(lag.reshape(1), *[h for h, _ in turned], *[l for _, l in turned], sketches)


def finish_kernel(chunks, inverse_ref, kept_ref, *refs):
    *received, out_ref = refs
    lags, chans, width = out_ref.shape
    size = lags // chunks
    inverse_high, inverse_low = split(inverse_ref[...].T)
    for n in range(chunks):
        part = slice(n * size, (n + 1) * size)
        total = kept_ref[part]
        for ref in received[n::chunks]:
            total = total + ref[...]
        high, low = split(total.reshape(size * chans, width))
        out_ref[part] = three(high, low, inverse_high, inverse_low).reshape(size, chans, width)


def finish(inverse, kept, received, chunks):
    lags, chans, width = kept.shape
    return pl.pallas_call(
        functools.partial(finish_kernel, chunks),
        in_specs=[VMEM] * (2 + len(received)),
        out_specs=VMEM,
        out_shape=jax.ShapeDtypeStruct(kept.shape, F32),
        compiler_params=pltpu.CompilerParams(vmem_limit_bytes=20 * 2**20),
        cost_estimate=cost(6 * lags * chans * width * width, 12 * lags * chans * width),
        name="finish",
    )(inverse, kept, *received)


def small(body, out_shapes, *args, smem=0):
    shapes = [jax.ShapeDtypeStruct(shape, F32) for shape in out_shapes]
    size = sum(a.size for a in args) + sum(s.size for s in shapes)
    outs = pl.pallas_call(
        body,
        in_specs=[SMEM] * smem + [VMEM] * (len(args) - smem),
        out_specs=[VMEM] * len(shapes),
        out_shape=shapes,
        compiler_params=pltpu.CompilerParams(vmem_limit_bytes=6 * 2**20),
        cost_estimate=cost(size, 4 * size),
    )(*args)
    return outs[0] if len(outs) == 1 else outs


def cut_kernel(record_ref, *outs):
    rows = record_ref.shape[0]
    before_ref, after_ref, *parts = outs
    rim = after_ref.shape[0]
    before_ref[...] = record_ref[rows - rim :]
    after_ref[...] = record_ref[:rim]
    first = 0
    for ref in parts:
        ref[...] = record_ref[first : first + ref.shape[0]]
        first += ref.shape[0]


def add_pair_kernel(keep_ref, got_ref, own_ref, pass_ref):
    own_ref[...] = keep_ref[:1] + got_ref[:1]
    pass_ref[...] = keep_ref[1:] + got_ref[1:]


def add_masked_kernel(rim, place_ref, own_ref, got_ref, out_ref):
    value = own_ref[...] + got_ref[...]
    row = lax.broadcasted_iota(jnp.int32, value.shape, 1)
    kept = (row >= rim) | (place_ref[0] > 0) | (place_ref[1] > 0)
    out_ref[...] = jnp.where(kept, value, 0.0)


def join_kernel(a_ref, b_ref, out_ref):
    out_ref[: a_ref.shape[0]] = a_ref[...]
    out_ref[a_ref.shape[0] :] = b_ref[...]


def add_kernel(a_ref, b_ref, out_ref):
    out_ref[...] = a_ref[...] + b_ref[...]


def joined(a, b):
    return small(join_kernel, [(a.shape[0] + b.shape[0],) + a.shape[1:]], a, b)


def added(a, b):
    return small(add_kernel, [a.shape], a, b)


def on_device(record, test_matrix):
    rows, chans = record.shape
    lags, _, width = test_matrix.shape
    n_time = lax.axis_size("tm")
    n_chan = lax.axis_size("chan")
    here = lax.axis_index("tm")
    mine = lax.axis_index("chan")
    half = n_time // 2
    mids = n_time // 4
    per = lags // n_time
    rim = lags
    place = jnp.stack([mine, here, mine % 2, mine // 2])

    def to(block, target, axis="tm"):
        count = lax.axis_size(axis)
        route = [(i, target(i)) for i in range(count) if 0 <= target(i) < count]
        return lax.ppermute(block, axis, route)

    def to_both(block, target):
        route = []
        for t in range(n_time):
            for c in range(n_chan):
                a, b = target(t, c)
                route.append((t * n_chan + c, a * n_chan + b))
        return lax.ppermute(block, ("tm", "chan"), route)

    def beside(t):
        return t ^ 1

    def across(t):
        return (t + half) % n_time

    cut = [0, rows // 2, 3 * rows // 4, rows]
    sizes = [rim, rim] + [b - a for a, b in zip(cut, cut[1:])]
    before, after, *parts = small(cut_kernel, [(n, chans) for n in sizes], record)
    before = to(before, lambda i: i + 1)
    after = to(after, lambda i: i - 1)
    beside_record = to(record, beside)
    across_parts = [to(part, across) for part in parts]
    both_parts = [to(part, beside) for part in across_parts]

    keep, give = sketch(place, before, record, after, test_matrix, n_chan)
    share = keep.shape[1]
    got = to(give, lambda i: i ^ 1, "chan")
    own, passed = small(add_pair_kernel, [(1, share, width)] * 2, keep, got)
    got = to(passed, lambda i: i ^ 2, "chan")
    own = small(functools.partial(add_masked_kernel, rim), [own.shape], place, own, got, smem=1)

    def even(c):
        return c % 2 == 0

    got = to_both(own, lambda t, c: (t, c ^ 2) if even(c) else (across(t), c))
    own = joined(own, got)
    got = to_both(own, lambda t, c: (across(t), c) if even(c) else (beside(t), c))
    own = joined(own, got)
    got = to_both(own, lambda t, c: (beside(t), c) if even(c) else (t, c ^ 2))
    own = joined(own, got)
    got = to(own, lambda i: i ^ 1, "chan")
    gram = gram_of(place, own, rim)
    distance = 2
    while distance < half:
        other = to(gram, lambda i: i ^ distance)
        gram = added(gram, other)
        distance *= 2
    gram_other = to(gram, lambda i: i ^ 1, "chan")
    sketches = assemble(place, own, got, n_chan)

    turned = [turn(record)]
    turned += [turn(p) for p in across_parts]
    turned += [turn(beside_record)]
    turned += [turn(p) for p in both_parts]
    places = [(0, 0, rim)] + [(1, a, rim) for a in cut[:-1]] + [(2, 0, rim)] + [(3, a, rim) for a in cut[:-1]]

    middle = (here % half) // 2
    outer = here - 2 * middle

    def owner_lag(step):
        return (outer + 2 * ((middle + step) % mids)) * per

    chunks = max(per // 2, 1)
    size = per // chunks
    received = []
    for s in range(1, mids):
        def route(i):
            m = (i % half) // 2
            return i - 2 * m + 2 * ((m + s) % mids)

        for n in range(chunks):
            part = lagged(owner_lag(s) + n * size, turned, places, sketches, size)
            received.append(to(part, route))
    kept = lagged(owner_lag(0), turned, places, sketches, per)
    inverse = factor(gram, gram_other)

    def whitened(x):
        return lax.dot_general(
            x, inverse, (((x.ndim - 1,), (1,)), ((), ())), precision=HIGHEST, preferred_element_type=F32
        )

    basis = whitened(sketches[0, rim:]) * jnp.sqrt(F32(rows * n_time))
    return basis, finish(inverse, kept, received, chunks)


def solution(mesh):
    return jax.shard_map(
        on_device,
        mesh=mesh,
        in_specs=(P("tm", "chan"), P(None, "chan", None)),
        out_specs=(P("tm", None), P("tm", "chan", None)),
        check_vma=False,
    )
```

```python
import functools

import jax
import jax.numpy as jnp
from jax import lax
from jax.experimental import pallas as pl
from jax.experimental.pallas import tpu as pltpu
from jax.sharding import PartitionSpec as P


F32 = jnp.float32
BF16 = jnp.bfloat16
HIGHEST = lax.Precision.HIGHEST
STEP = 16
SMEM = pl.BlockSpec(memory_space=pltpu.SMEM)
VMEM = pl.BlockSpec(memory_space=pltpu.VMEM)


def cost(flops, size):
    return pl.CostEstimate(flops=flops, bytes_accessed=size, transcendentals=0)


def split(x):
    high = x.astype(BF16)
    return high, (x - high.astype(F32)).astype(BF16)


def three(a_high, a_low, b_high, b_low):
    dot = functools.partial(jnp.dot, preferred_element_type=F32)
    return dot(a_high, b_high) + dot(a_high, b_low) + dot(a_low, b_high)


def sketch_kernel(place_ref, beside_ref, record_ref, beyond_ref, weight_ref, *refs):
    keep_ref, give_ref, high, low, even, odd, total, buffer, arrived = refs
    pair = pl.program_id(0)
    rows, width = total.shape
    groups = weight_ref.shape[0]

    def fetch(n):
        slot = lax.rem(n, 2)
        return pltpu.make_async_copy(weight_ref.at[:, pl.ds(2 * n, 2)], buffer.at[slot], arrived.at[slot])

    @pl.when(pair == 0)
    def _():
        fetch(pair).start()

    @pl.when(pair + 1 < pl.num_programs(0))
    def _():
        fetch(pair + 1).start()

    tiles = 3
    tile = (rows + STEP) // tiles

    @pl.when(pair == 0)
    def _():
        def place_rows(first, ref):
            part = slice(first, first + ref.shape[0])
            high[part], low[part] = split(ref[...])

        rim = beside_ref.shape[0]
        last = rim + record_ref.shape[0]
        place_rows(rim, record_ref)

        @pl.when(lax.rem(place_ref[1], 2) == 0)
        def _():
            place_rows(0, beyond_ref)
            place_rows(last, beside_ref)

        @pl.when(lax.rem(place_ref[1], 2) == 1)
        def _():
            place_rows(0, beside_ref)
            place_rows(last, beyond_ref)

        total[...] = jnp.zeros_like(total)

    fetch(pair).wait()
    slot = lax.rem(pair, 2)
    weight = jnp.concatenate(
        [jnp.concatenate([buffer[slot, a, 0], buffer[slot, a, 1]], axis=1) for a in range(groups)],
        axis=0,
    )
    weight_high, weight_low = split(weight)
    for first in range(0, tiles * tile, tile):
        starts = [first + a * STEP for a in range(groups)]
        left_high = jnp.concatenate([high[s : s + tile] for s in starts], axis=1)
        left_low = jnp.concatenate([low[s : s + tile] for s in starts], axis=1)
        value = three(left_high, left_low, weight_high, weight_low)
        even[first : first + tile] = value[:, :width]
        odd[first : first + tile] = value[:, width:]
    total[...] += even[pl.ds(2 * pair, rows), :] + odd[pl.ds(2 * pair + 1, rows), :]

    @pl.when(pair == pl.num_programs(0) - 1)
    def _():
        share = keep_ref.shape[1]
        for ref, flip in ((keep_ref, 0), (give_ref, 1)):
            for n in range(2):
                owner = jnp.bitwise_xor(place_ref[0], 2 * n + flip)
                ref[n] = total[pl.ds(pl.multiple_of(owner * share, 8), share), :]


def sketch(place, beside, record, beyond, weights, shares):
    lags, chans, width = weights.shape
    rows = beside.shape[0] + record.shape[0]
    length = rows + beyond.shape[0]
    share = rows // shares
    return pl.pallas_call(
        sketch_kernel,
        grid=(STEP // 2,),
        in_specs=[SMEM, VMEM, VMEM, VMEM, pl.BlockSpec(memory_space=pltpu.HBM)],
        out_specs=[VMEM] * 2,
        out_shape=[jax.ShapeDtypeStruct((2, share, width), F32)] * 2,
        scratch_shapes=[
            pltpu.VMEM((length, chans), BF16),
            pltpu.VMEM((length, chans), BF16),
            pltpu.VMEM((rows + STEP, width), F32),
            pltpu.VMEM((rows + STEP, width), F32),
            pltpu.VMEM((rows, width), F32),
            pltpu.VMEM((2, lags // STEP, 2, chans, width), F32),
            pltpu.SemaphoreType.DMA((2,)),
        ],
        compiler_params=pltpu.CompilerParams(vmem_limit_bytes=24 * 2**20),
        cost_estimate=cost(
            6 * rows * lags * chans * width,
            4 * (lags * chans * width + length * chans + rows * width),
        ),
        name="sketch",
    )(place, beside, record, beyond, pltpu.with_memory_space_constraint(weights.reshape(lags // STEP, STEP, chans, width), pltpu.HBM))


def turn_kernel(block_ref, high_ref, low_ref):
    high_ref[...], low_ref[...] = split(block_ref[...].T)


def turn(block):
    rows, chans = block.shape
    return pl.pallas_call(
        turn_kernel,
        in_specs=[VMEM],
        out_specs=[VMEM] * 2,
        out_shape=[jax.ShapeDtypeStruct((chans, rows), BF16)] * 2,
        compiler_params=pltpu.CompilerParams(vmem_limit_bytes=12 * 2**20),
        cost_estimate=cost(0, 8 * rows * chans),
        name="turn",
    )(block)


def assemble_kernel(place_ref, own_ref, got_ref, out_ref):
    pieces, share, _ = own_ref.shape
    blocks = pieces // 2
    low, high = place_ref[2], place_ref[3]

    def place(first_ref, second_ref):
        for b in range(blocks):
            for q in range(2):
                owner = 2 * jnp.bitwise_xor(high, q)
                first = pl.multiple_of(owner * share, 8)
                out_ref[b, pl.ds(first, share), :] = first_ref[2 * b + q]
                out_ref[b, pl.ds(pl.multiple_of(first + share, 8), share), :] = second_ref[blocks * q + b]

    @pl.when(low == 0)
    def _():
        place(own_ref, got_ref)

    @pl.when(low == 1)
    def _():
        place(got_ref, own_ref)


def assemble(place, own, got, shares):
    pieces, share, width = own.shape
    blocks = pieces // 2
    return pl.pallas_call(
        assemble_kernel,
        in_specs=[SMEM, VMEM, VMEM],
        out_specs=VMEM,
        out_shape=jax.ShapeDtypeStruct((blocks, shares * share, width), F32),
        compiler_params=pltpu.CompilerParams(vmem_limit_bytes=20 * 2**20),
        cost_estimate=cost(0, 8 * blocks * shares * share * width),
        name="assemble",
    )(place, own, got)


def gram_kernel(rim, place_ref, own_ref, out_ref):
    pieces, share, width = own_ref.shape
    blocks = pieces // 2
    low, high = place_ref[2], place_ref[3]
    kept = lax.broadcasted_iota(jnp.int32, (share, width), 0) >= rim

    def gram(value):
        return lax.dot_general(
            value, value, (((0,), (0,)), ((), ())), precision=HIGHEST, preferred_element_type=F32
        )

    @pl.when(low == 0)
    def _():
        halves = []
        for q in range(2):
            value = jnp.concatenate(
                [jnp.where(kept | (high != q), own_ref[2 * b + q], 0.0) for b in range(blocks)], axis=0
            )
            halves.append(gram(value))
        out_ref[...] = halves[0] + halves[1]

    @pl.when(low == 1)
    def _():
        halves = []
        for q in range(2):
            value = jnp.concatenate([own_ref[blocks * q + b] for b in range(blocks)], axis=0)
            halves.append(gram(value))
        out_ref[...] = halves[0] + halves[1]


def gram_of(place, own, rim):
    pieces, share, width = own.shape
    return pl.pallas_call(
        functools.partial(gram_kernel, rim),
        in_specs=[SMEM, VMEM],
        out_specs=VMEM,
        out_shape=jax.ShapeDtypeStruct((width, width), F32),
        compiler_params=pltpu.CompilerParams(vmem_limit_bytes=20 * 2**20),
        cost_estimate=cost(12 * pieces * share * width * width, 4 * pieces * share * width),
        name="gram",
    )(place, own)


def factor_kernel(gram_ref, other_ref, out_ref):
    size = gram_ref.shape[0]
    tile = 8
    tiles = [slice(q, q + tile) for q in range(0, size, tile)]
    row_of = lax.broadcasted_iota(jnp.int32, (tile, size), 0)
    col_of = lax.broadcasted_iota(jnp.int32, (tile, size), 1)
    g = [gram_ref[t, :] + other_ref[t, :] for t in tiles]
    x = [jnp.where(col_of == row_of + t.start, 1.0, 0.0).astype(F32) for t in tiles]
    for p, t in enumerate(tiles):
        first = t.start
        square = [
            [jnp.broadcast_to(g[p][a : a + 1, first + b : first + b + 1], (1, size)) for b in range(tile)]
            for a in range(tile)
        ]
        g_rows = [g[p][a : a + 1, :] for a in range(tile)]
        x_rows = [x[p][a : a + 1, :] for a in range(tile)]
        inverse, ratio = [], {}
        for a in range(tile):
            inverse.append(1.0 / square[a][a])
            for b in range(a + 1, tile):
                ratio[b, a] = square[a][b] * inverse[a]
                for c in range(b, tile):
                    square[b][c] = square[b][c] - ratio[b, a] * square[a][c]
                g_rows[b] = g_rows[b] - ratio[b, a] * g_rows[a]
                x_rows[b] = x_rows[b] - ratio[b, a] * x_rows[a]
        g_scaled = [v * i for v, i in zip(g_rows, inverse)]
        x_scaled = [v * i for v, i in zip(x_rows, inverse)]
        for q in range(p + 1, len(tiles)):
            columns = [
                jnp.broadcast_to(g[q][:, first + a : first + a + 1], (tile, size)) for a in range(tile)
            ]
            for a in range(tile):
                for b in range(a + 1, tile):
                    columns[b] = columns[b] - ratio[b, a] * columns[a]
            for a in range(tile):
                g[q] = g[q] - columns[a] * g_scaled[a]
                x[q] = x[q] - columns[a] * x_scaled[a]
        for a in range(tile):
            out_ref[first + a : first + a + 1, :] = x_rows[a] * (1.0 / jnp.sqrt(square[a][a]))


def factor(gram, other):
    return pl.pallas_call(
        factor_kernel,
        in_specs=[VMEM] * 2,
        out_specs=VMEM,
        out_shape=jax.ShapeDtypeStruct(gram.shape, F32),
        compiler_params=pltpu.CompilerParams(vmem_limit_bytes=8 * 2**20),
        cost_estimate=cost(3 * 10**9, 2**17),
        name="factor",
    )(gram, other)


def lagged_kernel(places, lag_ref, *refs):
    count = len(places)
    highs, lows, (sketch_ref, out_ref) = refs[:count], refs[count : 2 * count], refs[2 * count :]
    width = out_ref.shape[2]
    rim = places[0][2]
    start = rim - (lag_ref[0] + 2 * pl.program_id(0))
    total = jnp.zeros((out_ref.shape[1], 2 * width), F32)
    for (block, first, _), high, low in zip(places, highs, lows):
        rows = high.shape[1]
        moved = jnp.concatenate(
            [
                sketch_ref[block, pl.ds(start + first, rows), :],
                sketch_ref[block, pl.ds(start + first - 1, rows), :],
            ],
            axis=1,
        )
        moved_high, moved_low = split(moved)
        total = total + three(high[...], low[...], moved_high, moved_low)
    out_ref[0] = total[:, :width]
    out_ref[1] = total[:, width:]


def lagged(lag, turned, places, sketches, lags):
    blocks, length, width = sketches.shape
    chans = turned[0][0].shape[0]
    rows = sum(h.shape[1] for h, _ in turned)
    return pl.pallas_call(
        functools.partial(lagged_kernel, places),
        grid=(lags // 2,),
        in_specs=[SMEM] + [VMEM] * (2 * len(turned) + 1),
        out_specs=pl.BlockSpec((2, chans, width), lambda i: (i, 0, 0)),
        out_shape=jax.ShapeDtypeStruct((lags, chans, width), F32),
        compiler_params=pltpu.CompilerParams(vmem_limit_bytes=20 * 2**20),
        cost_estimate=cost(
            6 * rows * chans * lags * width,
            4 * (rows * chans + lags * chans * width + blocks * length * width),
        ),
        name="lagged",
    )(lag.reshape(1), *[h for h, _ in turned], *[l for _, l in turned], sketches)


def finish_kernel(chunks, inverse_ref, kept_ref, *refs):
    received, out_ref = refs[:chunks], refs[-1]
    size, chans, width = received[0].shape
    inverse_high, inverse_low = split(inverse_ref[...].T)
    for n, ref in enumerate(received):
        part = slice(n * size, (n + 1) * size)
        high, low = split((kept_ref[part] + ref[...]).reshape(size * chans, width))
        out_ref[part] = three(high, low, inverse_high, inverse_low).reshape(size, chans, width)


def finish(inverse, kept, received, first, out=None):
    _, chans, width = kept.shape
    size = received[0].shape[0]
    count = len(received)
    block = pl.BlockSpec((count * size, chans, width), lambda i: (first // count, 0, 0))
    extra = [] if out is None else [out]
    return pl.pallas_call(
        functools.partial(finish_kernel, count),
        grid=(1,),
        in_specs=[VMEM, block] + [VMEM] * count + [pl.BlockSpec(memory_space=pl.ANY)] * len(extra),
        out_specs=block,
        out_shape=jax.ShapeDtypeStruct(kept.shape, F32),
        input_output_aliases={} if out is None else {2 + count: 0},
        compiler_params=pltpu.CompilerParams(vmem_limit_bytes=12 * 2**20),
        cost_estimate=cost(6 * count * size * chans * width * width, 12 * count * size * chans * width),
        name="finish",
    )(inverse, kept, *received, *extra)


def small(body, out_shapes, *args, smem=0):
    shapes = [jax.ShapeDtypeStruct(shape, F32) for shape in out_shapes]
    size = sum(a.size for a in args) + sum(s.size for s in shapes)
    outs = pl.pallas_call(
        body,
        in_specs=[SMEM] * smem + [VMEM] * (len(args) - smem),
        out_specs=[VMEM] * len(shapes),
        out_shape=shapes,
        compiler_params=pltpu.CompilerParams(vmem_limit_bytes=6 * 2**20),
        cost_estimate=cost(size, 4 * size),
    )(*args)
    return outs[0] if len(outs) == 1 else outs


def cut_kernel(place_ref, record_ref, *outs):
    rows = record_ref.shape[0]
    beside_ref, beyond_ref, *parts = outs
    rim = beside_ref.shape[0]

    @pl.when(lax.rem(place_ref[1], 2) == 0)
    def _():
        beside_ref[...] = record_ref[rows - rim :]
        beyond_ref[...] = record_ref[:rim]

    @pl.when(lax.rem(place_ref[1], 2) == 1)
    def _():
        beside_ref[...] = record_ref[:rim]
        beyond_ref[...] = record_ref[rows - rim :]

    first = 0
    for ref in parts:
        ref[...] = record_ref[first : first + ref.shape[0]]
        first += ref.shape[0]


def add_pair_kernel(keep_ref, got_ref, own_ref, pass_ref):
    own_ref[...] = keep_ref[:1] + got_ref[:1]
    pass_ref[...] = keep_ref[1:] + got_ref[1:]


def add_masked_kernel(rim, place_ref, own_ref, got_ref, out_ref):
    value = own_ref[...] + got_ref[...]
    row = lax.broadcasted_iota(jnp.int32, value.shape, 1)
    kept = (row >= rim) | (place_ref[0] > 0) | (place_ref[1] > 0)
    out_ref[...] = jnp.where(kept, value, 0.0)


def join_kernel(a_ref, b_ref, out_ref):
    out_ref[: a_ref.shape[0]] = a_ref[...]
    out_ref[a_ref.shape[0] :] = b_ref[...]


def add_kernel(a_ref, b_ref, out_ref):
    out_ref[...] = a_ref[...] + b_ref[...]


def joined(a, b):
    return small(join_kernel, [(a.shape[0] + b.shape[0],) + a.shape[1:]], a, b)


def added(a, b):
    return small(add_kernel, [a.shape], a, b)


def on_device(record, test_matrix):
    rows, chans = record.shape
    lags, _, width = test_matrix.shape
    n_time = lax.axis_size("tm")
    n_chan = lax.axis_size("chan")
    here = lax.axis_index("tm")
    mine = lax.axis_index("chan")
    half = n_time // 2
    mids = n_time // 4
    per = lags // n_time
    rim = lags
    place = jnp.stack([mine, here, mine % 2, mine // 2])

    def to(block, target, axis="tm"):
        count = lax.axis_size(axis)
        route = [(i, target(i)) for i in range(count) if 0 <= target(i) < count]
        return lax.ppermute(block, axis, route)

    def to_both(block, target):
        route = []
        for t in range(n_time):
            for c in range(n_chan):
                a, b = target(t, c)
                route.append((t * n_chan + c, a * n_chan + b))
        return lax.ppermute(block, ("tm", "chan"), route)

    def beside(t):
        return t ^ 1

    def across(t):
        return (t + half) % n_time

    cut = [0, rows // 2, 3 * rows // 4, rows]
    sizes = [rim, rim] + [b - a for a, b in zip(cut, cut[1:])]
    at_beside, at_beyond, *parts = small(cut_kernel, [(n, chans) for n in sizes], place, record, smem=1)
    at_beyond = to(at_beyond, lambda i: i - 1 + 2 * (i % 2))
    at_beside = to(at_beside, beside)
    beside_record = to(record, beside)
    across_parts = [to(part, across) for part in parts]
    both_parts = [to(part, beside) for part in across_parts]

    keep, give = sketch(place, at_beside, record, at_beyond, test_matrix, n_chan)
    share = keep.shape[1]
    got = to(give, lambda i: i ^ 1, "chan")
    own, passed = small(add_pair_kernel, [(1, share, width)] * 2, keep, got)
    got = to(passed, lambda i: i ^ 2, "chan")
    own = small(functools.partial(add_masked_kernel, rim), [own.shape], place, own, got, smem=1)

    def even(c):
        return c % 2 == 0

    got = to_both(own, lambda t, c: (t, c ^ 2) if even(c) else (across(t), c))
    own = joined(own, got)
    got = to_both(own, lambda t, c: (across(t), c) if even(c) else (beside(t), c))
    own = joined(own, got)
    got = to_both(own, lambda t, c: (beside(t), c) if even(c) else (t, c ^ 2))
    own = joined(own, got)
    got = to(own, lambda i: i ^ 1, "chan")
    gram = gram_of(place, own, rim)
    distance = 2
    while distance < half:
        other = to(gram, lambda i: i ^ distance)
        gram = added(gram, other)
        distance *= 2
    gram_other = to(gram, lambda i: i ^ 1, "chan")
    sketches = assemble(place, own, got, n_chan)

    turned = [turn(record)]
    turned += [turn(p) for p in across_parts]
    turned += [turn(beside_record)]
    turned += [turn(p) for p in both_parts]
    places = [(0, 0, rim)] + [(1, a, rim) for a in cut[:-1]] + [(2, 0, rim)] + [(3, a, rim) for a in cut[:-1]]

    middle = (here % half) // 2
    outer = here - 2 * middle

    def owner_lag(step):
        return (outer + 2 * ((middle + step) % mids)) * per

    chunks = max(per // 2, 1)
    size = per // chunks
    received = []
    for s in range(1, mids):
        def route(i):
            m = (i % half) // 2
            return i - 2 * m + 2 * ((m + s) % mids)

        for n in range(chunks):
            part = lagged(owner_lag(s) + n * size, turned, places, sketches, size)
            received.append(to(part, route))
    kept = lagged(owner_lag(0), turned, places, sketches, per)
    inverse = factor(gram, gram_other)

    def whitened(x):
        return lax.dot_general(
            x, inverse, (((x.ndim - 1,), (1,)), ((), ())), precision=HIGHEST, preferred_element_type=F32
        )

    basis = whitened(sketches[0, rim:]) * jnp.sqrt(F32(rows * n_time))
    totals = []
    for n in range(chunks):
        total = received[n]
        for more in received[n + chunks :: chunks]:
            total = added(total, more)
        totals.append(total)
    coeffs = None
    for first, count in ((0, chunks // 2), (chunks // 2, chunks // 4), (3 * chunks // 4, chunks - 3 * chunks // 4)):
        if count:
            coeffs = finish(inverse, kept, totals[first : first + count], first, coeffs)
    return basis, coeffs


def solution(mesh):
    return jax.shard_map(
        on_device,
        mesh=mesh,
        in_specs=(P("tm", "chan"), P(None, "chan", None)),
        out_specs=(P("tm", None), P("tm", "chan", None)),
        check_vma=False,
    )
```

```python
import functools

import jax
import jax.numpy as jnp
from jax import lax
from jax.experimental import pallas as pl
from jax.experimental.pallas import tpu as pltpu
from jax.sharding import PartitionSpec as P


F32 = jnp.float32
BF16 = jnp.bfloat16
HIGHEST = lax.Precision.HIGHEST
STEP = 16
SMEM = pl.BlockSpec(memory_space=pltpu.SMEM)
VMEM = pl.BlockSpec(memory_space=pltpu.VMEM)


def cost(flops, size):
    return pl.CostEstimate(flops=flops, bytes_accessed=size, transcendentals=0)


def split(x):
    high = x.astype(BF16)
    return high, (x - high.astype(F32)).astype(BF16)


def three(a_high, a_low, b_high, b_low):
    dot = functools.partial(jnp.dot, preferred_element_type=F32)
    return dot(a_high, b_high) + dot(a_high, b_low) + dot(a_low, b_high)


def sketch_kernel(place_ref, record_ref, weight_ref, *refs):
    keep_ref, give_ref, high, low, even, odd, total, buffer, arrived = refs
    pair = pl.program_id(0)
    rows, width = total.shape
    groups = weight_ref.shape[0]

    def fetch(n):
        slot = lax.rem(n, 2)
        return pltpu.make_async_copy(weight_ref.at[:, pl.ds(2 * n, 2)], buffer.at[slot], arrived.at[slot])

    @pl.when(pair == 0)
    def _():
        fetch(pair).start()

    @pl.when(pair + 1 < pl.num_programs(0))
    def _():
        fetch(pair + 1).start()

    tiles = 3
    tile = (rows + STEP) // tiles

    @pl.when(pair == 0)
    def _():
        rim = rows - record_ref.shape[0]
        last = high.shape[0] - rim
        for ref, value in ((high, 0), (low, 1)):
            ref[:rim] = jnp.zeros((rim, ref.shape[1]), BF16)
            ref[last:] = jnp.zeros((rim, ref.shape[1]), BF16)
            ref[rim:last] = split(record_ref[...])[value]
        total[...] = jnp.zeros_like(total)

    fetch(pair).wait()
    slot = lax.rem(pair, 2)
    weight = jnp.concatenate(
        [jnp.concatenate([buffer[slot, a, 0], buffer[slot, a, 1]], axis=1) for a in range(groups)],
        axis=0,
    )
    weight_high, weight_low = split(weight)
    for first in range(0, tiles * tile, tile):
        starts = [first + a * STEP for a in range(groups)]
        left_high = jnp.concatenate([high[s : s + tile] for s in starts], axis=1)
        left_low = jnp.concatenate([low[s : s + tile] for s in starts], axis=1)
        value = three(left_high, left_low, weight_high, weight_low)
        even[first : first + tile] = value[:, :width]
        odd[first : first + tile] = value[:, width:]
    total[...] += even[pl.ds(2 * pair, rows), :] + odd[pl.ds(2 * pair + 1, rows), :]

    @pl.when(pair == pl.num_programs(0) - 1)
    def _():
        share = keep_ref.shape[1]
        for ref, flip in ((keep_ref, 0), (give_ref, 1)):
            for n in range(2):
                owner = jnp.bitwise_xor(place_ref[0], 2 * n + flip)
                ref[n] = total[pl.ds(pl.multiple_of(owner * share, 8), share), :]


def sketch(place, record, weights, shares):
    lags, chans, width = weights.shape
    rows = lags + record.shape[0]
    length = rows + lags
    share = rows // shares
    return pl.pallas_call(
        sketch_kernel,
        grid=(STEP // 2,),
        in_specs=[SMEM, VMEM, pl.BlockSpec(memory_space=pltpu.HBM)],
        out_specs=[VMEM] * 2,
        out_shape=[jax.ShapeDtypeStruct((2, share, width), F32)] * 2,
        scratch_shapes=[
            pltpu.VMEM((length, chans), BF16),
            pltpu.VMEM((length, chans), BF16),
            pltpu.VMEM((rows + STEP, width), F32),
            pltpu.VMEM((rows + STEP, width), F32),
            pltpu.VMEM((rows, width), F32),
            pltpu.VMEM((2, lags // STEP, 2, chans, width), F32),
            pltpu.SemaphoreType.DMA((2,)),
        ],
        compiler_params=pltpu.CompilerParams(vmem_limit_bytes=24 * 2**20),
        cost_estimate=cost(
            6 * rows * lags * chans * width,
            4 * (lags * chans * width + length * chans + rows * width),
        ),
        name="sketch",
    )(
        place,
        record,
        pltpu.with_memory_space_constraint(
            weights.reshape(lags // STEP, STEP, chans, width), pltpu.HBM
        ),
    )


def turn_kernel(block_ref, high_ref, low_ref):
    high_ref[...], low_ref[...] = split(block_ref[...].T)


def turn(block):
    rows, chans = block.shape
    return pl.pallas_call(
        turn_kernel,
        in_specs=[VMEM],
        out_specs=[VMEM] * 2,
        out_shape=[jax.ShapeDtypeStruct((chans, rows), BF16)] * 2,
        compiler_params=pltpu.CompilerParams(vmem_limit_bytes=12 * 2**20),
        cost_estimate=cost(0, 8 * rows * chans),
        name="turn",
    )(block)


def even_piece(block, pair):
    return 4 * (block // 2) + 2 * pair + block % 2


def assemble_kernel(mids, place_ref, own_ref, got_ref, edge_own_ref, edge_got_ref, out_ref):
    _, share, _ = own_ref.shape
    blocks, rim, _ = edge_own_ref.shape
    low, high, outer, middle = place_ref[2], place_ref[3], place_ref[5], place_ref[6]
    end = out_ref.shape[1] - rim

    def place(first_ref, second_ref):
        for b in range(blocks):
            for q in range(2):
                owner = 2 * jnp.bitwise_xor(high, q)
                first = pl.multiple_of(owner * share, 8)
                out_ref[b, pl.ds(first, share), :] = first_ref[even_piece(b, q)]
                out_ref[b, pl.ds(pl.multiple_of(first + share, 8), share), :] = second_ref[blocks * q + b]

    def edges(inner, heads_ref, tails_ref):
        for z in range(2):
            left, right = (z, z + 2) if inner == 0 else (z + 2, z)
            side = jnp.bitwise_xor(outer, z)
            value = out_ref[left, end:] + out_ref[right, :rim]
            out_ref[left, end:] = value
            out_ref[right, :rim] = value
            tail = 2 * (1 - inner)
            value = jnp.where(middle > 0, tails_ref[tail + z], tails_ref[tail + 1 - z])
            some = (middle > 0) | (side == 1)
            out_ref[left, :rim] = jnp.where(some, out_ref[left, :rim] + value, 0.0)
            head = 2 * inner
            value = jnp.where(middle < mids - 1, heads_ref[head + z], heads_ref[head + 1 - z])
            some = (middle < mids - 1) | (side == 0)
            out_ref[right, end:] = out_ref[right, end:] + jnp.where(some, value, 0.0)

    @pl.when(low == 0)
    def _():
        place(own_ref, got_ref)

    @pl.when(low == 1)
    def _():
        place(got_ref, own_ref)

    for inner in range(2):

        @pl.when((place_ref[4] == inner) & (low == 0))
        def _():
            edges(inner, edge_own_ref, edge_got_ref)

        @pl.when((place_ref[4] == inner) & (low == 1))
        def _():
            edges(inner, edge_got_ref, edge_own_ref)


def assemble(place, own, got, edge_own, edge_got, shares, mids):
    pieces, share, width = own.shape
    blocks = pieces // 2
    return pl.pallas_call(
        functools.partial(assemble_kernel, mids),
        in_specs=[SMEM, VMEM, VMEM, VMEM, VMEM],
        out_specs=VMEM,
        out_shape=jax.ShapeDtypeStruct((blocks, shares * share, width), F32),
        compiler_params=pltpu.CompilerParams(vmem_limit_bytes=12 * 2**20),
        cost_estimate=cost(0, 8 * blocks * shares * share * width),
        name="assemble",
    )(place, own, got, edge_own, edge_got)


def gram_kernel(rim, place_ref, own_ref, out_ref):
    pieces, share, width = own_ref.shape
    blocks = pieces // 2
    low, high = place_ref[2], place_ref[3]
    row = lax.broadcasted_iota(jnp.int32, (share, width), 0)

    def gram(value):
        return lax.dot_general(
            value, value, (((0,), (0,)), ((), ())), precision=HIGHEST, preferred_element_type=F32
        )

    def both(kept, piece):
        halves = []
        for q in range(2):
            value = jnp.concatenate(
                [jnp.where(kept(q), own_ref[piece(b, q)], 0.0) for b in range(blocks)], axis=0
            )
            halves.append(gram(value))
        out_ref[...] = halves[0] + halves[1]

    @pl.when(low == 0)
    def _():
        both(lambda q: (row >= rim) | (high != q), even_piece)

    @pl.when(low == 1)
    def _():
        both(lambda q: (row < share - rim) | (high == q), lambda b, q: blocks * q + b)


def gram_of(place, own, rim):
    pieces, share, width = own.shape
    return pl.pallas_call(
        functools.partial(gram_kernel, rim),
        in_specs=[SMEM, VMEM],
        out_specs=VMEM,
        out_shape=jax.ShapeDtypeStruct((width, width), F32),
        compiler_params=pltpu.CompilerParams(vmem_limit_bytes=20 * 2**20),
        cost_estimate=cost(12 * pieces * share * width * width, 4 * pieces * share * width),
        name="gram",
    )(place, own)


def factor_kernel(gram_ref, other_ref, out_ref):
    size = gram_ref.shape[0]
    tile = 8
    tiles = [slice(q, q + tile) for q in range(0, size, tile)]
    row_of = lax.broadcasted_iota(jnp.int32, (tile, size), 0)
    col_of = lax.broadcasted_iota(jnp.int32, (tile, size), 1)
    g = [gram_ref[t, :] + other_ref[t, :] for t in tiles]
    x = [jnp.where(col_of == row_of + t.start, 1.0, 0.0).astype(F32) for t in tiles]
    for p, t in enumerate(tiles):
        first = t.start
        square = [
            [jnp.broadcast_to(g[p][a : a + 1, first + b : first + b + 1], (1, size)) for b in range(tile)]
            for a in range(tile)
        ]
        g_rows = [g[p][a : a + 1, :] for a in range(tile)]
        x_rows = [x[p][a : a + 1, :] for a in range(tile)]
        inverse, ratio = [], {}
        for a in range(tile):
            inverse.append(1.0 / square[a][a])
            for b in range(a + 1, tile):
                ratio[b, a] = square[a][b] * inverse[a]
                for c in range(b, tile):
                    square[b][c] = square[b][c] - ratio[b, a] * square[a][c]
                g_rows[b] = g_rows[b] - ratio[b, a] * g_rows[a]
                x_rows[b] = x_rows[b] - ratio[b, a] * x_rows[a]
        g_scaled = [v * i for v, i in zip(g_rows, inverse)]
        x_scaled = [v * i for v, i in zip(x_rows, inverse)]
        for q in range(p + 1, len(tiles)):
            columns = [
                jnp.broadcast_to(g[q][:, first + a : first + a + 1], (tile, size)) for a in range(tile)
            ]
            for a in range(tile):
                for b in range(a + 1, tile):
                    columns[b] = columns[b] - ratio[b, a] * columns[a]
            for a in range(tile):
                g[q] = g[q] - columns[a] * g_scaled[a]
                x[q] = x[q] - columns[a] * x_scaled[a]
        for a in range(tile):
            out_ref[first + a : first + a + 1, :] = x_rows[a] * (1.0 / jnp.sqrt(square[a][a]))


def factor(gram, other):
    return pl.pallas_call(
        factor_kernel,
        in_specs=[VMEM] * 2,
        out_specs=VMEM,
        out_shape=jax.ShapeDtypeStruct(gram.shape, F32),
        compiler_params=pltpu.CompilerParams(vmem_limit_bytes=8 * 2**20),
        cost_estimate=cost(3 * 10**9, 2**17),
        name="factor",
    )(gram, other)


def lagged_kernel(places, lag_ref, *refs):
    count = len(places)
    highs, lows, (sketch_ref, out_ref) = refs[:count], refs[count : 2 * count], refs[2 * count :]
    width = out_ref.shape[2]
    rim = places[0][2]
    start = rim - (lag_ref[0] + 2 * pl.program_id(0))
    total = jnp.zeros((out_ref.shape[1], 2 * width), F32)
    for (block, first, _), high, low in zip(places, highs, lows):
        rows = high.shape[1]
        moved = jnp.concatenate(
            [
                sketch_ref[block, pl.ds(start + first, rows), :],
                sketch_ref[block, pl.ds(start + first - 1, rows), :],
            ],
            axis=1,
        )
        moved_high, moved_low = split(moved)
        total = total + three(high[...], low[...], moved_high, moved_low)
    out_ref[0] = total[:, :width]
    out_ref[1] = total[:, width:]


def lagged(lag, turned, places, sketches, lags):
    blocks, length, width = sketches.shape
    chans = turned[0][0].shape[0]
    rows = sum(h.shape[1] for h, _ in turned)
    return pl.pallas_call(
        functools.partial(lagged_kernel, places),
        grid=(lags // 2,),
        in_specs=[SMEM] + [VMEM] * (2 * len(turned) + 1),
        out_specs=pl.BlockSpec((2, chans, width), lambda i: (i, 0, 0)),
        out_shape=jax.ShapeDtypeStruct((lags, chans, width), F32),
        compiler_params=pltpu.CompilerParams(vmem_limit_bytes=20 * 2**20),
        cost_estimate=cost(
            6 * rows * chans * lags * width,
            4 * (rows * chans + lags * chans * width + blocks * length * width),
        ),
        name="lagged",
    )(lag.reshape(1), *[h for h, _ in turned], *[l for _, l in turned], sketches)


def finish_kernel(chunks, inverse_ref, kept_ref, *refs):
    received, out_ref = refs[:chunks], refs[-1]
    size, chans, width = received[0].shape
    inverse_high, inverse_low = split(inverse_ref[...].T)
    for n, ref in enumerate(received):
        part = slice(n * size, (n + 1) * size)
        high, low = split((kept_ref[part] + ref[...]).reshape(size * chans, width))
        out_ref[part] = three(high, low, inverse_high, inverse_low).reshape(size, chans, width)


def finish(inverse, kept, received, first, out=None):
    _, chans, width = kept.shape
    size = received[0].shape[0]
    count = len(received)
    block = pl.BlockSpec((count * size, chans, width), lambda i: (first // count, 0, 0))
    extra = [] if out is None else [out]
    return pl.pallas_call(
        functools.partial(finish_kernel, count),
        grid=(1,),
        in_specs=[VMEM, block] + [VMEM] * count + [pl.BlockSpec(memory_space=pl.ANY)] * len(extra),
        out_specs=block,
        out_shape=jax.ShapeDtypeStruct(kept.shape, F32),
        input_output_aliases={} if out is None else {2 + count: 0},
        compiler_params=pltpu.CompilerParams(vmem_limit_bytes=12 * 2**20),
        cost_estimate=cost(6 * count * size * chans * width * width, 12 * count * size * chans * width),
        name="finish",
    )(inverse, kept, *received, *extra)


def small(body, out_shapes, *args, smem=0):
    shapes = [jax.ShapeDtypeStruct(shape, F32) for shape in out_shapes]
    size = sum(a.size for a in args) + sum(s.size for s in shapes)
    outs = pl.pallas_call(
        body,
        in_specs=[SMEM] * smem + [VMEM] * (len(args) - smem),
        out_specs=[VMEM] * len(shapes),
        out_shape=shapes,
        compiler_params=pltpu.CompilerParams(vmem_limit_bytes=8 * 2**20),
        cost_estimate=cost(size, 4 * size),
    )(*args)
    return outs[0] if len(outs) == 1 else outs


def cut_kernel(record_ref, *parts):
    first = 0
    for ref in parts:
        ref[...] = record_ref[first : first + ref.shape[0]]
        first += ref.shape[0]


def add_pair_kernel(keep_ref, got_ref, own_ref, pass_ref):
    own_ref[0] = keep_ref[0] + got_ref[0]
    pass_ref[0] = keep_ref[1] + got_ref[1]


def join_edges_kernel(place_ref, a_ref, b_ref, out_ref, edge_ref):
    join_kernel(a_ref, b_ref, out_ref)
    blocks, rim, _ = edge_ref.shape
    share = a_ref.shape[1]
    for high in range(2):

        @pl.when((place_ref[2] == 0) & (place_ref[3] == high))
        def _():
            for b in range(blocks):
                edge_ref[b] = out_ref[even_piece(b, high), :rim]

        @pl.when((place_ref[2] == 1) & (place_ref[3] == high))
        def _():
            for b in range(blocks):
                edge_ref[b] = out_ref[blocks * (1 - high) + b, share - rim :]


def edge_gram_kernel(rim, sketch_ref, a_ref, b_ref, out_ref):
    blocks, length, _ = sketch_ref.shape
    value = jnp.concatenate([sketch_ref[b, length - rim :] for b in range(blocks)], axis=0)
    out_ref[...] = (a_ref[...] + b_ref[...]) + lax.dot_general(
        value, value, (((0,), (0,)), ((), ())), precision=HIGHEST, preferred_element_type=F32
    )


def join_kernel(a_ref, b_ref, out_ref):
    out_ref[: a_ref.shape[0]] = a_ref[...]
    out_ref[a_ref.shape[0] :] = b_ref[...]


def add_kernel(a_ref, b_ref, out_ref):
    out_ref[...] = a_ref[...] + b_ref[...]


def joined(a, b):
    return small(join_kernel, [(a.shape[0] + b.shape[0],) + a.shape[1:]], a, b)


def added(a, b):
    return small(add_kernel, [a.shape], a, b)


def on_device(record, test_matrix):
    rows, chans = record.shape
    lags, _, width = test_matrix.shape
    n_time = lax.axis_size("tm")
    n_chan = lax.axis_size("chan")
    here = lax.axis_index("tm")
    mine = lax.axis_index("chan")
    half = n_time // 2
    mids = n_time // 4
    per = lags // n_time
    rim = lags
    place = jnp.stack(
        [mine, here, mine % 2, mine // 2, here % 2, here // half, (here % half) // 2]
    ).astype(jnp.int32)

    def to(block, target, axis="tm"):
        count = lax.axis_size(axis)
        route = [(i, target(i)) for i in range(count) if 0 <= target(i) < count]
        return lax.ppermute(block, axis, route)

    def to_both(block, target):
        route = []
        for t in range(n_time):
            for c in range(n_chan):
                a, b = target(t, c)
                if 0 <= a < n_time:
                    route.append((t * n_chan + c, a * n_chan + b))
        return lax.ppermute(block, ("tm", "chan"), route)

    def even(c):
        return c % 2 == 0

    def beside(t):
        return t ^ 1

    def across(t):
        return (t + half) % n_time

    cut = [0, rows // 2, 3 * rows // 4, rows]
    parts = small(cut_kernel, [(b - a, chans) for a, b in zip(cut, cut[1:])], record)
    beside_record = to(record, beside)
    across_parts = [to(part, across) for part in parts]
    both_parts = [to(part, beside) for part in across_parts]

    keep, give = sketch(place, record, test_matrix, n_chan)
    share = keep.shape[1]
    got = to(give, lambda i: i ^ 1, "chan")
    own, passed = small(add_pair_kernel, [(1, share, width)] * 2, keep, got)
    own = added(own, to(passed, lambda i: i ^ 2, "chan"))

    own = joined(own, to_both(own, lambda t, c: (across(t), c)))
    got = to_both(own, lambda t, c: (t, c ^ 2) if even(c) else (beside(t), c))
    own = joined(own, got)
    got = to_both(own, lambda t, c: (beside(t), c) if even(c) else (t, c ^ 2))
    own, edge = small(
        join_edges_kernel, [(2 * own.shape[0], share, width), (own.shape[0], rim, width)], place, own, got, smem=1
    )
    got = to(own, lambda i: i ^ 1, "chan")

    def neighbour(t, step):
        middle = (t % half) // 2
        return t - 2 * middle + 2 * ((middle + step) % mids)

    edge = to_both(edge, lambda t, c: (neighbour(t, -1 if even(c) else 1), c))
    edge_got = to(edge, lambda i: i ^ 1, "chan")
    gram = gram_of(place, own, rim)
    gram_got = to(gram, lambda i: i ^ 1, "chan")
    sketches = assemble(place, own, got, edge, edge_got, n_chan, mids)
    gram = small(functools.partial(edge_gram_kernel, rim), [gram.shape], sketches, gram, gram_got)
    other = jnp.zeros_like(gram)
    distance = 2
    while distance < half:
        if distance > 2:
            gram = added(gram, other)
        other = to(gram, lambda i: i ^ distance)
        distance *= 2

    turned = [turn(record)]
    turned += [turn(p) for p in across_parts]
    turned += [turn(beside_record)]
    turned += [turn(p) for p in both_parts]
    places = [(0, 0, rim)] + [(1, a, rim) for a in cut[:-1]] + [(2, 0, rim)] + [(3, a, rim) for a in cut[:-1]]

    middle = (here % half) // 2
    outer = here - 2 * middle

    def owner_lag(step):
        return (outer + 2 * ((middle + step) % mids)) * per

    chunks = max(per // 2, 1)
    size = per // chunks
    received = []
    for s in range(1, mids):
        def route(i):
            return neighbour(i, s)

        for n in range(chunks):
            part = lagged(owner_lag(s) + n * size, turned, places, sketches, size)
            received.append(to(part, route))
    kept = lagged(owner_lag(0), turned, places, sketches, per)
    inverse = factor(gram, other)

    def whitened(x):
        return lax.dot_general(
            x, inverse, (((x.ndim - 1,), (1,)), ((), ())), precision=HIGHEST, preferred_element_type=F32
        )

    basis = whitened(sketches[0, rim:]) * jnp.sqrt(F32(rows * n_time))
    totals = []
    for n in range(chunks):
        total = received[n]
        for more in received[n + chunks :: chunks]:
            total = added(total, more)
        totals.append(total)
    coeffs = None
    for first, count in ((0, chunks // 2), (chunks // 2, chunks // 4), (3 * chunks // 4, chunks - 3 * chunks // 4)):
        if count:
            coeffs = finish(inverse, kept, totals[first : first + count], first, coeffs)
    return basis, coeffs


def solution(mesh):
    return jax.shard_map(
        on_device,
        mesh=mesh,
        in_specs=(P("tm", "chan"), P(None, "chan", None)),
        out_specs=(P("tm", None), P("tm", "chan", None)),
        check_vma=False,
    )
```

```python
import functools

import jax
import jax.numpy as jnp
from jax import lax
from jax.experimental import pallas as pl
from jax.experimental.pallas import tpu as pltpu
from jax.sharding import PartitionSpec as P


F32 = jnp.float32
BF16 = jnp.bfloat16
HIGHEST = lax.Precision.HIGHEST
STEP = 16
SMEM = pl.BlockSpec(memory_space=pltpu.SMEM)
VMEM = pl.BlockSpec(memory_space=pltpu.VMEM)


def cost(flops, size):
    return pl.CostEstimate(flops=flops, bytes_accessed=size, transcendentals=0)


def split(x):
    high = x.astype(BF16)
    return high, (x - high.astype(F32)).astype(BF16)


def three(a_high, a_low, b_high, b_low):
    dot = functools.partial(jnp.dot, preferred_element_type=F32)
    return dot(a_high, b_high) + dot(a_high, b_low) + dot(a_low, b_high)


def sketch_kernel(place_ref, record_ref, weight_ref, *refs):
    keep_ref, give_ref, high, low, even, odd, total, buffer, arrived = refs
    pair = pl.program_id(0)
    rows, width = total.shape
    groups = weight_ref.shape[0]

    def fetch(n):
        slot = lax.rem(n, 2)
        return pltpu.make_async_copy(weight_ref.at[:, pl.ds(2 * n, 2)], buffer.at[slot], arrived.at[slot])

    @pl.when(pair == 0)
    def _():
        fetch(pair).start()

    @pl.when(pair + 1 < pl.num_programs(0))
    def _():
        fetch(pair + 1).start()

    tiles = 3
    tile = (rows + STEP) // tiles

    @pl.when(pair == 0)
    def _():
        rim = rows - record_ref.shape[0]
        last = high.shape[0] - rim
        for ref, value in ((high, 0), (low, 1)):
            ref[:rim] = jnp.zeros((rim, ref.shape[1]), BF16)
            ref[last:] = jnp.zeros((rim, ref.shape[1]), BF16)
            ref[rim:last] = split(record_ref[...])[value]
        total[...] = jnp.zeros_like(total)

    fetch(pair).wait()
    slot = lax.rem(pair, 2)
    weight = jnp.concatenate(
        [jnp.concatenate([buffer[slot, a, 0], buffer[slot, a, 1]], axis=1) for a in range(groups)],
        axis=0,
    )
    weight_high, weight_low = split(weight)
    for first in range(0, tiles * tile, tile):
        starts = [first + a * STEP for a in range(groups)]
        left_high = jnp.concatenate([high[s : s + tile] for s in starts], axis=1)
        left_low = jnp.concatenate([low[s : s + tile] for s in starts], axis=1)
        value = three(left_high, left_low, weight_high, weight_low)
        even[first : first + tile] = value[:, :width]
        odd[first : first + tile] = value[:, width:]
    total[...] += even[pl.ds(2 * pair, rows), :] + odd[pl.ds(2 * pair + 1, rows), :]

    @pl.when(pair == pl.num_programs(0) - 1)
    def _():
        share = keep_ref.shape[1]
        for ref, flip in ((keep_ref, 0), (give_ref, 1)):
            for n in range(2):
                owner = jnp.bitwise_xor(place_ref[0], 2 * n + flip)
                ref[n] = total[pl.ds(pl.multiple_of(owner * share, 8), share), :]


def sketch(place, record, weights, shares):
    lags, chans, width = weights.shape
    rows = lags + record.shape[0]
    length = rows + lags
    share = rows // shares
    return pl.pallas_call(
        sketch_kernel,
        grid=(STEP // 2,),
        in_specs=[SMEM, VMEM, pl.BlockSpec(memory_space=pltpu.HBM)],
        out_specs=[VMEM] * 2,
        out_shape=[jax.ShapeDtypeStruct((2, share, width), F32)] * 2,
        scratch_shapes=[
            pltpu.VMEM((length, chans), BF16),
            pltpu.VMEM((length, chans), BF16),
            pltpu.VMEM((rows + STEP, width), F32),
            pltpu.VMEM((rows + STEP, width), F32),
            pltpu.VMEM((rows, width), F32),
            pltpu.VMEM((2, lags // STEP, 2, chans, width), F32),
            pltpu.SemaphoreType.DMA((2,)),
        ],
        compiler_params=pltpu.CompilerParams(vmem_limit_bytes=24 * 2**20),
        cost_estimate=cost(
            6 * rows * lags * chans * width,
            4 * (lags * chans * width + length * chans + rows * width),
        ),
        name="sketch",
    )(
        place,
        record,
        pltpu.with_memory_space_constraint(
            weights.reshape(lags // STEP, STEP, chans, width), pltpu.HBM
        ),
    )


def turn_kernel(*refs):
    count = len(refs) // 3
    for n in range(count):
        refs[count + 2 * n][...], refs[count + 2 * n + 1][...] = split(refs[n][...].T)


def turn(blocks):
    size = sum(b.size for b in blocks)
    outs = pl.pallas_call(
        turn_kernel,
        in_specs=[VMEM] * len(blocks),
        out_specs=[VMEM] * (2 * len(blocks)),
        out_shape=[jax.ShapeDtypeStruct(b.shape[::-1], BF16) for b in blocks for _ in range(2)],
        compiler_params=pltpu.CompilerParams(vmem_limit_bytes=12 * 2**20),
        cost_estimate=cost(0, 8 * size),
        name="turn",
    )(*blocks)
    return list(zip(outs[::2], outs[1::2]))


def even_piece(block, pair):
    return 4 * (block // 2) + 2 * pair + block % 2


def assemble_kernel(mids, place_ref, own_ref, got_ref, edge_own_ref, edge_got_ref, out_ref):
    _, share, _ = own_ref.shape
    blocks, rim, _ = edge_own_ref.shape
    low, high, outer, middle = place_ref[2], place_ref[3], place_ref[5], place_ref[6]
    end = out_ref.shape[1] - rim

    def place(first_ref, second_ref):
        for b in range(blocks):
            for q in range(2):
                owner = 2 * jnp.bitwise_xor(high, q)
                first = pl.multiple_of(owner * share, 8)
                out_ref[b, pl.ds(first, share), :] = first_ref[even_piece(b, q)]
                out_ref[b, pl.ds(pl.multiple_of(first + share, 8), share), :] = second_ref[blocks * q + b]

    def edges(inner, heads_ref, tails_ref):
        for z in range(2):
            left, right = (z, z + 2) if inner == 0 else (z + 2, z)
            side = jnp.bitwise_xor(outer, z)
            value = out_ref[left, end:] + out_ref[right, :rim]
            out_ref[left, end:] = value
            out_ref[right, :rim] = value
            tail = 2 * (1 - inner)
            value = jnp.where(middle > 0, tails_ref[tail + z], tails_ref[tail + 1 - z])
            some = (middle > 0) | (side == 1)
            out_ref[left, :rim] = jnp.where(some, out_ref[left, :rim] + value, 0.0)
            head = 2 * inner
            value = jnp.where(middle < mids - 1, heads_ref[head + z], heads_ref[head + 1 - z])
            some = (middle < mids - 1) | (side == 0)
            out_ref[right, end:] = out_ref[right, end:] + jnp.where(some, value, 0.0)

    @pl.when(low == 0)
    def _():
        place(own_ref, got_ref)

    @pl.when(low == 1)
    def _():
        place(got_ref, own_ref)

    for inner in range(2):

        @pl.when((place_ref[4] == inner) & (low == 0))
        def _():
            edges(inner, edge_own_ref, edge_got_ref)

        @pl.when((place_ref[4] == inner) & (low == 1))
        def _():
            edges(inner, edge_got_ref, edge_own_ref)


def assemble(place, own, got, edge_own, edge_got, shares, mids):
    pieces, share, width = own.shape
    blocks = pieces // 2
    return pl.pallas_call(
        functools.partial(assemble_kernel, mids),
        in_specs=[SMEM, VMEM, VMEM, VMEM, VMEM],
        out_specs=VMEM,
        out_shape=jax.ShapeDtypeStruct((blocks, shares * share, width), F32),
        compiler_params=pltpu.CompilerParams(vmem_limit_bytes=12 * 2**20),
        cost_estimate=cost(0, 8 * blocks * shares * share * width),
        name="assemble",
    )(place, own, got, edge_own, edge_got)


def gram_kernel(rim, place_ref, own_ref, out_ref):
    pieces, share, width = own_ref.shape
    blocks = pieces // 2
    low, high = place_ref[2], place_ref[3]
    row = lax.broadcasted_iota(jnp.int32, (share, width), 0)

    def gram(value):
        return lax.dot_general(
            value, value, (((0,), (0,)), ((), ())), precision=HIGHEST, preferred_element_type=F32
        )

    def both(kept, piece):
        halves = []
        for q in range(2):
            value = jnp.concatenate(
                [jnp.where(kept(q), own_ref[piece(b, q)], 0.0) for b in range(blocks)], axis=0
            )
            halves.append(gram(value))
        out_ref[...] = halves[0] + halves[1]

    @pl.when(low == 0)
    def _():
        both(lambda q: (row >= rim) | (high != q), even_piece)

    @pl.when(low == 1)
    def _():
        both(lambda q: (row < share - rim) | (high == q), lambda b, q: blocks * q + b)


def gram_of(place, own, rim):
    pieces, share, width = own.shape
    return pl.pallas_call(
        functools.partial(gram_kernel, rim),
        in_specs=[SMEM, VMEM],
        out_specs=VMEM,
        out_shape=jax.ShapeDtypeStruct((width, width), F32),
        compiler_params=pltpu.CompilerParams(vmem_limit_bytes=20 * 2**20),
        cost_estimate=cost(12 * pieces * share * width * width, 4 * pieces * share * width),
        name="gram",
    )(place, own)


def factor_kernel(gram_ref, other_ref, out_ref):
    size = gram_ref.shape[0]
    tile = 8
    tiles = [slice(q, q + tile) for q in range(0, size, tile)]
    row_of = lax.broadcasted_iota(jnp.int32, (tile, size), 0)
    col_of = lax.broadcasted_iota(jnp.int32, (tile, size), 1)
    g = [gram_ref[t, :] + other_ref[t, :] for t in tiles]
    x = [jnp.where(col_of == row_of + t.start, 1.0, 0.0).astype(F32) for t in tiles]
    for p, t in enumerate(tiles):
        first = t.start
        square = [
            [jnp.broadcast_to(g[p][a : a + 1, first + b : first + b + 1], (1, size)) for b in range(tile)]
            for a in range(tile)
        ]
        g_rows = [g[p][a : a + 1, :] for a in range(tile)]
        x_rows = [x[p][a : a + 1, :] for a in range(tile)]
        inverse, ratio = [], {}
        for a in range(tile):
            inverse.append(1.0 / square[a][a])
            for b in range(a + 1, tile):
                ratio[b, a] = square[a][b] * inverse[a]
                for c in range(b, tile):
                    square[b][c] = square[b][c] - ratio[b, a] * square[a][c]
                g_rows[b] = g_rows[b] - ratio[b, a] * g_rows[a]
                x_rows[b] = x_rows[b] - ratio[b, a] * x_rows[a]
        g_scaled = [v * i for v, i in zip(g_rows, inverse)]
        x_scaled = [v * i for v, i in zip(x_rows, inverse)]
        for q in range(p + 1, len(tiles)):
            columns = [
                jnp.broadcast_to(g[q][:, first + a : first + a + 1], (tile, size)) for a in range(tile)
            ]
            for a in range(tile):
                for b in range(a + 1, tile):
                    columns[b] = columns[b] - ratio[b, a] * columns[a]
            for a in range(tile):
                g[q] = g[q] - columns[a] * g_scaled[a]
                x[q] = x[q] - columns[a] * x_scaled[a]
        for a in range(tile):
            out_ref[first + a : first + a + 1, :] = x_rows[a] * (1.0 / jnp.sqrt(square[a][a]))


def factor(gram, other):
    return pl.pallas_call(
        factor_kernel,
        in_specs=[VMEM] * 2,
        out_specs=VMEM,
        out_shape=jax.ShapeDtypeStruct(gram.shape, F32),
        compiler_params=pltpu.CompilerParams(vmem_limit_bytes=8 * 2**20),
        cost_estimate=cost(3 * 10**9, 2**17),
        name="factor",
    )(gram, other)


def lagged_kernel(places, lag_ref, *refs):
    count = len(places)
    highs, lows, (sketch_ref, out_ref) = refs[:count], refs[count : 2 * count], refs[2 * count :]
    width = out_ref.shape[2]
    rim = places[0][2]
    start = rim - (lag_ref[0] + 2 * pl.program_id(0))
    total = jnp.zeros((out_ref.shape[1], 2 * width), F32)
    for (block, first, _), high, low in zip(places, highs, lows):
        rows = high.shape[1]
        moved = jnp.concatenate(
            [
                sketch_ref[block, pl.ds(start + first, rows), :],
                sketch_ref[block, pl.ds(start + first - 1, rows), :],
            ],
            axis=1,
        )
        moved_high, moved_low = split(moved)
        total = total + three(high[...], low[...], moved_high, moved_low)
    out_ref[0] = total[:, :width]
    out_ref[1] = total[:, width:]


def lagged(lag, turned, places, sketches, lags):
    blocks, length, width = sketches.shape
    chans = turned[0][0].shape[0]
    rows = sum(h.shape[1] for h, _ in turned)
    return pl.pallas_call(
        functools.partial(lagged_kernel, places),
        grid=(lags // 2,),
        in_specs=[SMEM] + [VMEM] * (2 * len(turned) + 1),
        out_specs=pl.BlockSpec((2, chans, width), lambda i: (i, 0, 0)),
        out_shape=jax.ShapeDtypeStruct((lags, chans, width), F32),
        compiler_params=pltpu.CompilerParams(vmem_limit_bytes=20 * 2**20),
        cost_estimate=cost(
            6 * rows * chans * lags * width,
            4 * (rows * chans + lags * chans * width + blocks * length * width),
        ),
        name="lagged",
    )(lag.reshape(1), *[h for h, _ in turned], *[l for _, l in turned], sketches)


def finish_kernel(inverse_ref, kept_ref, *refs):
    out_ref = refs[-1]
    size, chans, width = out_ref.shape
    inverse_high, inverse_low = split(inverse_ref[...].T)

    def put(received_ref):
        high, low = split((kept_ref[...] + received_ref[...]).reshape(size * chans, width))
        out_ref[...] = three(high, low, inverse_high, inverse_low).reshape(size, chans, width)

    for n in range(pl.num_programs(0)):

        @pl.when(pl.program_id(0) == n)
        def _():
            put(refs[n])


def finish(inverse, kept, received, first, out=None):
    _, chans, width = kept.shape
    size = received[0].shape[0]
    count = len(received)
    block = pl.BlockSpec((size, chans, width), lambda i: (first + i, 0, 0))
    extra = [] if out is None else [out]
    return pl.pallas_call(
        finish_kernel,
        grid=(count,),
        in_specs=[VMEM, block] + [VMEM] * count + [pl.BlockSpec(memory_space=pl.ANY)] * len(extra),
        out_specs=block,
        out_shape=jax.ShapeDtypeStruct(kept.shape, F32),
        input_output_aliases={} if out is None else {2 + count: 0},
        compiler_params=pltpu.CompilerParams(vmem_limit_bytes=12 * 2**20),
        cost_estimate=cost(6 * count * size * chans * width * width, 12 * count * size * chans * width),
        name="finish",
    )(inverse, kept, *received, *extra)


def small(body, out_shapes, *args, smem=0):
    shapes = [jax.ShapeDtypeStruct(shape, F32) for shape in out_shapes]
    size = sum(a.size for a in args) + sum(s.size for s in shapes)
    outs = pl.pallas_call(
        body,
        in_specs=[SMEM] * smem + [VMEM] * (len(args) - smem),
        out_specs=[VMEM] * len(shapes),
        out_shape=shapes,
        compiler_params=pltpu.CompilerParams(vmem_limit_bytes=8 * 2**20),
        cost_estimate=cost(size, 4 * size),
    )(*args)
    return outs[0] if len(outs) == 1 else outs


def cut_kernel(record_ref, *refs):
    *parts, arrived = refs
    copies, first = [], 0
    for n, ref in enumerate(parts):
        rows = pl.ds(first, ref.shape[0])
        copies.append(pltpu.make_async_copy(record_ref.at[rows], ref, arrived.at[n]))
        first += ref.shape[0]
    for copy in copies:
        copy.start()
    for copy in copies:
        copy.wait()


def cut_up(record, sizes):
    chans = record.shape[1]
    return pl.pallas_call(
        cut_kernel,
        in_specs=[pl.BlockSpec(memory_space=pltpu.HBM)],
        out_specs=[VMEM] * len(sizes),
        out_shape=[jax.ShapeDtypeStruct((n, chans), F32) for n in sizes],
        scratch_shapes=[pltpu.SemaphoreType.DMA((len(sizes),))],
        compiler_params=pltpu.CompilerParams(vmem_limit_bytes=4 * 2**20),
        cost_estimate=cost(0, 8 * record.size),
        name="cut",
    )(record)


def add_pair_kernel(keep_ref, got_ref, own_ref, pass_ref):
    own_ref[0] = keep_ref[0] + got_ref[0]
    pass_ref[0] = keep_ref[1] + got_ref[1]


def edges_kernel(place_ref, own_ref, edge_ref):
    blocks, rim, _ = edge_ref.shape
    share = own_ref.shape[1]
    for high in range(2):

        @pl.when((place_ref[2] == 0) & (place_ref[3] == high))
        def _():
            for b in range(blocks):
                edge_ref[b] = own_ref[even_piece(b, high), :rim]

        @pl.when((place_ref[2] == 1) & (place_ref[3] == high))
        def _():
            for b in range(blocks):
                edge_ref[b] = own_ref[blocks * (1 - high) + b, share - rim :]


def edge_gram_kernel(rim, sketch_ref, a_ref, b_ref, out_ref):
    blocks, length, _ = sketch_ref.shape
    value = jnp.concatenate([sketch_ref[b, length - rim :] for b in range(blocks)], axis=0)
    out_ref[...] = (a_ref[...] + b_ref[...]) + lax.dot_general(
        value, value, (((0,), (0,)), ((), ())), precision=HIGHEST, preferred_element_type=F32
    )


def basis_kernel(root, inverse_ref, sketch_ref, out_ref):
    rim = sketch_ref.shape[1] - out_ref.shape[0]
    value = three(*split(sketch_ref[0, rim:]), *split(inverse_ref[...].T))
    out_ref[...] = value * root


def join_kernel(a_ref, b_ref, out_ref):
    out_ref[: a_ref.shape[0]] = a_ref[...]
    out_ref[a_ref.shape[0] :] = b_ref[...]


def add_kernel(a_ref, b_ref, out_ref):
    out_ref[...] = a_ref[...] + b_ref[...]


def joined(a, b):
    return small(join_kernel, [(a.shape[0] + b.shape[0],) + a.shape[1:]], a, b)


def added(a, b):
    return small(add_kernel, [a.shape], a, b)


def on_device(record, test_matrix):
    rows, _ = record.shape
    lags, _, width = test_matrix.shape
    n_time = lax.axis_size("tm")
    n_chan = lax.axis_size("chan")
    here = lax.axis_index("tm")
    mine = lax.axis_index("chan")
    half = n_time // 2
    mids = n_time // 4
    per = lags // n_time
    rim = lags
    place = jnp.stack(
        [mine, here, mine % 2, mine // 2, here % 2, here // half, (here % half) // 2]
    ).astype(jnp.int32)

    def to(block, target, axis="tm"):
        count = lax.axis_size(axis)
        route = [(i, target(i)) for i in range(count) if 0 <= target(i) < count]
        return lax.ppermute(block, axis, route)

    def to_both(block, target):
        route = []
        for t in range(n_time):
            for c in range(n_chan):
                a, b = target(t, c)
                if 0 <= a < n_time:
                    route.append((t * n_chan + c, a * n_chan + b))
        return lax.ppermute(block, ("tm", "chan"), route)

    def even(c):
        return c % 2 == 0

    def beside(t):
        return t ^ 1

    def across(t):
        return (t + half) % n_time

    cut = [0, rows // 2, 3 * rows // 4, rows]
    parts = cut_up(record, [b - a for a, b in zip(cut, cut[1:])])
    beside_record = to(record, beside)
    across_parts = [to(part, across) for part in parts]
    both_parts = [to(part, beside) for part in across_parts]

    keep, give = sketch(place, record, test_matrix, n_chan)
    share = keep.shape[1]
    got = to(give, lambda i: i ^ 1, "chan")
    own, passed = small(add_pair_kernel, [(1, share, width)] * 2, keep, got)
    own = added(own, to(passed, lambda i: i ^ 2, "chan"))

    own = joined(own, to_both(own, lambda t, c: (across(t), c)))
    got = to_both(own, lambda t, c: (t, c ^ 2) if even(c) else (beside(t), c))
    own = joined(own, got)
    got = to_both(own, lambda t, c: (beside(t), c) if even(c) else (t, c ^ 2))
    own = joined(own, got)
    edge = small(edges_kernel, [(own.shape[0] // 2, rim, width)], place, own, smem=1)
    got = to(own, lambda i: i ^ 1, "chan")

    def neighbour(t, step):
        middle = (t % half) // 2
        return t - 2 * middle + 2 * ((middle + step) % mids)

    edge = to_both(edge, lambda t, c: (neighbour(t, -1 if even(c) else 1), c))
    edge_got = to(edge, lambda i: i ^ 1, "chan")
    gram = gram_of(place, own, rim)
    gram_got = to(gram, lambda i: i ^ 1, "chan")
    sketches = assemble(place, own, got, edge, edge_got, n_chan, mids)
    gram = small(functools.partial(edge_gram_kernel, rim), [gram.shape], sketches, gram, gram_got)
    other = jnp.zeros_like(gram)
    distance = 2
    while distance < half:
        if distance > 2:
            gram = added(gram, other)
        other = to(gram, lambda i: i ^ distance)
        distance *= 2

    early = turn([record, beside_record, *across_parts[:2], both_parts[0]])
    late = turn([across_parts[2], *both_parts[1:]])
    turned = [early[0], early[2], early[3], late[0], early[1], early[4], late[1], late[2]]
    places = [(0, 0, rim)] + [(1, a, rim) for a in cut[:-1]] + [(2, 0, rim)] + [(3, a, rim) for a in cut[:-1]]

    middle = (here % half) // 2
    outer = here - 2 * middle

    def owner_lag(step):
        return (outer + 2 * ((middle + step) % mids)) * per

    chunks = max(per // 2, 1)
    size = per // chunks
    received = []
    for s in range(1, mids):
        def route(i):
            return neighbour(i, s)

        for n in range(chunks):
            part = lagged(owner_lag(s) + n * size, turned, places, sketches, size)
            received.append(to(part, route))
    kept = lagged(owner_lag(0), turned, places, sketches, per)
    inverse = factor(gram, other)

    basis = small(
        functools.partial(basis_kernel, float(rows * n_time) ** 0.5),
        [(rows, width)],
        inverse,
        sketches,
    )
    totals = []
    for n in range(chunks):
        total = received[n]
        for more in received[n + chunks :: chunks]:
            total = added(total, more)
        totals.append(total)
    coeffs = None
    for first, count in ((0, chunks - 1), (chunks - 1, 1)):
        if count:
            coeffs = finish(inverse, kept, totals[first : first + count], first, coeffs)
    return basis, coeffs


def solution(mesh):
    return jax.shard_map(
        on_device,
        mesh=mesh,
        in_specs=(P("tm", "chan"), P(None, "chan", None)),
        out_specs=(P("tm", None), P("tm", "chan", None)),
        check_vma=False,
    )
```

```python
import functools

import jax
import jax.numpy as jnp
from jax import lax
from jax.experimental import pallas as pl
from jax.experimental.pallas import tpu as pltpu
from jax.sharding import PartitionSpec as P


F32 = jnp.float32
BF16 = jnp.bfloat16
HIGHEST = lax.Precision.HIGHEST
STEP = 16
LAGS = 4
SMEM = pl.BlockSpec(memory_space=pltpu.SMEM)
VMEM = pl.BlockSpec(memory_space=pltpu.VMEM)


def cost(flops, size):
    return pl.CostEstimate(flops=flops, bytes_accessed=size, transcendentals=0)


def split(x):
    high = x.astype(BF16)
    return high, (x - high.astype(F32)).astype(BF16)


def three(a_high, a_low, b_high, b_low):
    dot = functools.partial(jnp.dot, preferred_element_type=F32)
    return dot(a_high, b_high) + dot(a_high, b_low) + dot(a_low, b_high)


def sketch_kernel(place_ref, record_ref, weight_ref, *refs):
    keep_ref, give_ref, high, low, sums, total, buffer, arrived = refs
    pair = pl.program_id(0)
    rows, width = total.shape
    groups = weight_ref.shape[0]

    lags = buffer.shape[2]

    def fetch(n):
        slot = lax.rem(n, 2)
        return pltpu.make_async_copy(
            weight_ref.at[:, pl.ds(lags * n, lags)], buffer.at[slot], arrived.at[slot]
        )

    @pl.when(pair == 0)
    def _():
        fetch(pair).start()

    @pl.when(pair + 1 < pl.num_programs(0))
    def _():
        fetch(pair + 1).start()

    tiles = 3
    tile = (rows + STEP) // tiles

    @pl.when(pair == 0)
    def _():
        rim = rows - record_ref.shape[0]
        last = high.shape[0] - rim
        for ref, value in ((high, 0), (low, 1)):
            ref[:rim] = jnp.zeros((rim, ref.shape[1]), BF16)
            ref[last:] = jnp.zeros((rim, ref.shape[1]), BF16)
            ref[rim:last] = split(record_ref[...])[value]
        total[...] = jnp.zeros_like(total)

    fetch(pair).wait()
    slot = lax.rem(pair, 2)
    weights = []
    for lag in range(0, lags, 2):
        weight = [
            jnp.concatenate([buffer[slot, a, lag], buffer[slot, a, lag + 1]], axis=1) for a in range(groups)
        ]
        weights.append(split(jnp.concatenate(weight, axis=0)))
    for first in range(0, tiles * tile, tile):
        starts = [first + a * STEP for a in range(groups)]
        left_high = jnp.concatenate([high[s : s + tile] for s in starts], axis=1)
        left_low = jnp.concatenate([low[s : s + tile] for s in starts], axis=1)
        for n, weight in enumerate(weights):
            value = three(left_high, left_low, *weight)
            sums[2 * n, first : first + tile] = value[:, :width]
            sums[2 * n + 1, first : first + tile] = value[:, width:]
    value = total[...]
    for n in range(lags):
        value = value + sums[n, pl.ds(lags * pair + n, rows), :]
    total[...] = value

    @pl.when(pair == pl.num_programs(0) - 1)
    def _():
        share = keep_ref.shape[1]
        for ref, flip in ((keep_ref, 0), (give_ref, 1)):
            for n in range(2):
                owner = jnp.bitwise_xor(place_ref[0], 2 * n + flip)
                ref[n] = total[pl.ds(pl.multiple_of(owner * share, 8), share), :]


def sketch(place, record, weights, shares):
    lags, chans, width = weights.shape
    rows = lags + record.shape[0]
    length = rows + lags
    share = rows // shares
    return pl.pallas_call(
        sketch_kernel,
        grid=(STEP // LAGS,),
        in_specs=[SMEM, VMEM, pl.BlockSpec(memory_space=pltpu.HBM)],
        out_specs=[VMEM] * 2,
        out_shape=[jax.ShapeDtypeStruct((2, share, width), F32)] * 2,
        scratch_shapes=[
            pltpu.VMEM((length, chans), BF16),
            pltpu.VMEM((length, chans), BF16),
            pltpu.VMEM((LAGS, rows + STEP, width), F32),
            pltpu.VMEM((rows, width), F32),
            pltpu.VMEM((2, lags // STEP, LAGS, chans, width), F32),
            pltpu.SemaphoreType.DMA((2,)),
        ],
        compiler_params=pltpu.CompilerParams(vmem_limit_bytes=24 * 2**20),
        cost_estimate=cost(
            6 * rows * lags * chans * width,
            4 * (lags * chans * width + length * chans + rows * width),
        ),
        name="sketch",
    )(
        place,
        record,
        pltpu.with_memory_space_constraint(
            weights.reshape(lags // STEP, STEP, chans, width), pltpu.HBM
        ),
    )


def turn_kernel(*refs):
    count = len(refs) // 3
    for n in range(count):
        refs[count + 2 * n][...], refs[count + 2 * n + 1][...] = split(refs[n][...].T)


def turn(blocks):
    size = sum(b.size for b in blocks)
    outs = pl.pallas_call(
        turn_kernel,
        in_specs=[VMEM] * len(blocks),
        out_specs=[VMEM] * (2 * len(blocks)),
        out_shape=[jax.ShapeDtypeStruct(b.shape[::-1], BF16) for b in blocks for _ in range(2)],
        compiler_params=pltpu.CompilerParams(vmem_limit_bytes=12 * 2**20),
        cost_estimate=cost(0, 8 * size),
        name="turn",
    )(*blocks)
    return list(zip(outs[::2], outs[1::2]))


def even_piece(block, pair):
    return 4 * (block // 2) + 2 * pair + block % 2


def assemble_kernel(mids, place_ref, own_ref, got_ref, edge_own_ref, edge_got_ref, out_ref):
    _, share, _ = own_ref.shape
    blocks, rim, _ = edge_own_ref.shape
    low, high, outer, middle = place_ref[2], place_ref[3], place_ref[5], place_ref[6]
    end = out_ref.shape[1] - rim

    def place(first_ref, second_ref):
        for b in range(blocks):
            for q in range(2):
                owner = 2 * jnp.bitwise_xor(high, q)
                first = pl.multiple_of(owner * share, 8)
                out_ref[b, pl.ds(first, share), :] = first_ref[even_piece(b, q)]
                out_ref[b, pl.ds(pl.multiple_of(first + share, 8), share), :] = second_ref[blocks * q + b]

    def edges(inner, heads_ref, tails_ref):
        for z in range(2):
            left, right = (z, z + 2) if inner == 0 else (z + 2, z)
            side = jnp.bitwise_xor(outer, z)
            value = out_ref[left, end:] + out_ref[right, :rim]
            out_ref[left, end:] = value
            out_ref[right, :rim] = value
            tail = 2 * (1 - inner)
            value = jnp.where(middle > 0, tails_ref[tail + z], tails_ref[tail + 1 - z])
            some = (middle > 0) | (side == 1)
            out_ref[left, :rim] = jnp.where(some, out_ref[left, :rim] + value, 0.0)
            head = 2 * inner
            value = jnp.where(middle < mids - 1, heads_ref[head + z], heads_ref[head + 1 - z])
            some = (middle < mids - 1) | (side == 0)
            out_ref[right, end:] = out_ref[right, end:] + jnp.where(some, value, 0.0)

    @pl.when(low == 0)
    def _():
        place(own_ref, got_ref)

    @pl.when(low == 1)
    def _():
        place(got_ref, own_ref)

    for inner in range(2):

        @pl.when((place_ref[4] == inner) & (low == 0))
        def _():
            edges(inner, edge_own_ref, edge_got_ref)

        @pl.when((place_ref[4] == inner) & (low == 1))
        def _():
            edges(inner, edge_got_ref, edge_own_ref)


def assemble(place, own, got, edge_own, edge_got, shares, mids):
    pieces, share, width = own.shape
    blocks = pieces // 2
    return pl.pallas_call(
        functools.partial(assemble_kernel, mids),
        in_specs=[SMEM, VMEM, VMEM, VMEM, VMEM],
        out_specs=VMEM,
        out_shape=jax.ShapeDtypeStruct((blocks, shares * share, width), F32),
        compiler_params=pltpu.CompilerParams(vmem_limit_bytes=12 * 2**20),
        cost_estimate=cost(0, 8 * blocks * shares * share * width),
        name="assemble",
    )(place, own, got, edge_own, edge_got)


def gram_kernel(rim, place_ref, own_ref, out_ref):
    pieces, share, width = own_ref.shape
    blocks = pieces // 2
    low, high = place_ref[2], place_ref[3]
    row = lax.broadcasted_iota(jnp.int32, (share, width), 0)

    def gram(value):
        return lax.dot_general(
            value, value, (((0,), (0,)), ((), ())), precision=HIGHEST, preferred_element_type=F32
        )

    def both(kept, piece):
        halves = []
        for q in range(2):
            value = jnp.concatenate(
                [jnp.where(kept(q), own_ref[piece(b, q)], 0.0) for b in range(blocks)], axis=0
            )
            halves.append(gram(value))
        out_ref[...] = halves[0] + halves[1]

    @pl.when(low == 0)
    def _():
        both(lambda q: (row >= rim) | (high != q), even_piece)

    @pl.when(low == 1)
    def _():
        both(lambda q: (row < share - rim) | (high == q), lambda b, q: blocks * q + b)


def gram_of(place, own, rim):
    pieces, share, width = own.shape
    return pl.pallas_call(
        functools.partial(gram_kernel, rim),
        in_specs=[SMEM, VMEM],
        out_specs=VMEM,
        out_shape=jax.ShapeDtypeStruct((width, width), F32),
        compiler_params=pltpu.CompilerParams(vmem_limit_bytes=20 * 2**20),
        cost_estimate=cost(12 * pieces * share * width * width, 4 * pieces * share * width),
        name="gram",
    )(place, own)


def factor_kernel(gram_ref, other_ref, out_ref):
    size = gram_ref.shape[0]
    tile = 8
    tiles = [slice(q, q + tile) for q in range(0, size, tile)]
    row_of = lax.broadcasted_iota(jnp.int32, (tile, size), 0)
    col_of = lax.broadcasted_iota(jnp.int32, (tile, size), 1)
    g = [gram_ref[t, :] + other_ref[t, :] for t in tiles]
    x = [jnp.where(col_of == row_of + t.start, 1.0, 0.0).astype(F32) for t in tiles]
    for p, t in enumerate(tiles):
        first = t.start
        square = [
            [jnp.broadcast_to(g[p][a : a + 1, first + b : first + b + 1], (1, size)) for b in range(tile)]
            for a in range(tile)
        ]
        g_rows = [g[p][a : a + 1, :] for a in range(tile)]
        x_rows = [x[p][a : a + 1, :] for a in range(tile)]
        inverse, ratio = [], {}
        for a in range(tile):
            inverse.append(1.0 / square[a][a])
            for b in range(a + 1, tile):
                ratio[b, a] = square[a][b] * inverse[a]
                for c in range(b, tile):
                    square[b][c] = square[b][c] - ratio[b, a] * square[a][c]
                g_rows[b] = g_rows[b] - ratio[b, a] * g_rows[a]
                x_rows[b] = x_rows[b] - ratio[b, a] * x_rows[a]
        g_scaled = [v * i for v, i in zip(g_rows, inverse)]
        x_scaled = [v * i for v, i in zip(x_rows, inverse)]
        for q in range(p + 1, len(tiles)):
            columns = [
                jnp.broadcast_to(g[q][:, first + a : first + a + 1], (tile, size)) for a in range(tile)
            ]
            for a in range(tile):
                for b in range(a + 1, tile):
                    columns[b] = columns[b] - ratio[b, a] * columns[a]
            for a in range(tile):
                g[q] = g[q] - columns[a] * g_scaled[a]
                x[q] = x[q] - columns[a] * x_scaled[a]
        for a in range(tile):
            out_ref[first + a : first + a + 1, :] = x_rows[a] * (1.0 / jnp.sqrt(square[a][a]))


def factor(gram, other):
    return pl.pallas_call(
        factor_kernel,
        in_specs=[VMEM] * 2,
        out_specs=VMEM,
        out_shape=jax.ShapeDtypeStruct(gram.shape, F32),
        compiler_params=pltpu.CompilerParams(vmem_limit_bytes=8 * 2**20),
        cost_estimate=cost(3 * 10**9, 2**17),
        name="factor",
    )(gram, other)


def lagged_kernel(places, lag_ref, *refs):
    count = len(places)
    highs, lows, (sketch_ref, out_ref) = refs[:count], refs[count : 2 * count], refs[2 * count :]
    width = out_ref.shape[2]
    rim = places[0][2]
    start = rim - (lag_ref[0] + 2 * pl.program_id(0))
    total = jnp.zeros((out_ref.shape[1], 2 * width), F32)
    for (block, first, _), high, low in zip(places, highs, lows):
        rows = high.shape[1]
        moved = jnp.concatenate(
            [
                sketch_ref[block, pl.ds(start + first, rows), :],
                sketch_ref[block, pl.ds(start + first - 1, rows), :],
            ],
            axis=1,
        )
        moved_high, moved_low = split(moved)
        total = total + three(high[...], low[...], moved_high, moved_low)
    out_ref[0] = total[:, :width]
    out_ref[1] = total[:, width:]


def lagged(lag, turned, places, sketches, lags):
    blocks, length, width = sketches.shape
    chans = turned[0][0].shape[0]
    rows = sum(h.shape[1] for h, _ in turned)
    return pl.pallas_call(
        functools.partial(lagged_kernel, places),
        grid=(lags // 2,),
        in_specs=[SMEM] + [VMEM] * (2 * len(turned) + 1),
        out_specs=pl.BlockSpec((2, chans, width), lambda i: (i, 0, 0)),
        out_shape=jax.ShapeDtypeStruct((lags, chans, width), F32),
        compiler_params=pltpu.CompilerParams(vmem_limit_bytes=20 * 2**20),
        cost_estimate=cost(
            6 * rows * chans * lags * width,
            4 * (rows * chans + lags * chans * width + blocks * length * width),
        ),
        name="lagged",
    )(lag.reshape(1), *[h for h, _ in turned], *[l for _, l in turned], sketches)


def finish_kernel(inverse_ref, kept_ref, *refs):
    out_ref = refs[-1]
    size, chans, width = out_ref.shape
    inverse_high, inverse_low = split(inverse_ref[...].T)

    def put(received_ref):
        high, low = split((kept_ref[...] + received_ref[...]).reshape(size * chans, width))
        out_ref[...] = three(high, low, inverse_high, inverse_low).reshape(size, chans, width)

    for n in range(pl.num_programs(0)):

        @pl.when(pl.program_id(0) == n)
        def _():
            put(refs[n])


def finish(inverse, kept, received, first, out=None):
    _, chans, width = kept.shape
    size = received[0].shape[0]
    count = len(received)
    block = pl.BlockSpec((size, chans, width), lambda i: (first + i, 0, 0))
    extra = [] if out is None else [out]
    return pl.pallas_call(
        finish_kernel,
        grid=(count,),
        in_specs=[VMEM, block] + [VMEM] * count + [pl.BlockSpec(memory_space=pl.ANY)] * len(extra),
        out_specs=block,
        out_shape=jax.ShapeDtypeStruct(kept.shape, F32),
        input_output_aliases={} if out is None else {2 + count: 0},
        compiler_params=pltpu.CompilerParams(vmem_limit_bytes=12 * 2**20),
        cost_estimate=cost(6 * count * size * chans * width * width, 12 * count * size * chans * width),
        name="finish",
    )(inverse, kept, *received, *extra)


def small(body, out_shapes, *args, smem=0):
    shapes = [jax.ShapeDtypeStruct(shape, F32) for shape in out_shapes]
    size = sum(a.size for a in args) + sum(s.size for s in shapes)
    outs = pl.pallas_call(
        body,
        in_specs=[SMEM] * smem + [VMEM] * (len(args) - smem),
        out_specs=[VMEM] * len(shapes),
        out_shape=shapes,
        compiler_params=pltpu.CompilerParams(vmem_limit_bytes=8 * 2**20),
        cost_estimate=cost(size, 4 * size),
    )(*args)
    return outs[0] if len(outs) == 1 else outs


def cut_kernel(record_ref, *refs):
    *parts, arrived = refs
    copies, first = [], 0
    for n, ref in enumerate(parts):
        rows = pl.ds(first, ref.shape[0])
        copies.append(pltpu.make_async_copy(record_ref.at[rows], ref, arrived.at[n]))
        first += ref.shape[0]
    for copy in copies:
        copy.start()
    for copy in copies:
        copy.wait()


def cut_up(record, sizes):
    chans = record.shape[1]
    return pl.pallas_call(
        cut_kernel,
        in_specs=[pl.BlockSpec(memory_space=pltpu.HBM)],
        out_specs=[VMEM] * len(sizes),
        out_shape=[jax.ShapeDtypeStruct((n, chans), F32) for n in sizes],
        scratch_shapes=[pltpu.SemaphoreType.DMA((len(sizes),))],
        compiler_params=pltpu.CompilerParams(vmem_limit_bytes=4 * 2**20),
        cost_estimate=cost(0, 8 * record.size),
        name="cut",
    )(record)


def add_pair_kernel(keep_ref, got_ref, own_ref, pass_ref):
    own_ref[0] = keep_ref[0] + got_ref[0]
    pass_ref[0] = keep_ref[1] + got_ref[1]


def edges_kernel(place_ref, own_ref, edge_ref):
    blocks, rim, _ = edge_ref.shape
    share = own_ref.shape[1]
    for high in range(2):

        @pl.when((place_ref[2] == 0) & (place_ref[3] == high))
        def _():
            for b in range(blocks):
                edge_ref[b] = own_ref[even_piece(b, high), :rim]

        @pl.when((place_ref[2] == 1) & (place_ref[3] == high))
        def _():
            for b in range(blocks):
                edge_ref[b] = own_ref[blocks * (1 - high) + b, share - rim :]


def edge_gram_kernel(rim, sketch_ref, a_ref, b_ref, out_ref):
    blocks, length, _ = sketch_ref.shape
    value = jnp.concatenate([sketch_ref[b, length - rim :] for b in range(blocks)], axis=0)
    out_ref[...] = (a_ref[...] + b_ref[...]) + lax.dot_general(
        value, value, (((0,), (0,)), ((), ())), precision=HIGHEST, preferred_element_type=F32
    )


def basis_kernel(root, inverse_ref, sketch_ref, out_ref):
    rim = sketch_ref.shape[1] - out_ref.shape[0]
    value = three(*split(sketch_ref[0, rim:]), *split(inverse_ref[...].T))
    out_ref[...] = value * root


def join_kernel(a_ref, b_ref, out_ref):
    out_ref[: a_ref.shape[0]] = a_ref[...]
    out_ref[a_ref.shape[0] :] = b_ref[...]


def add_kernel(a_ref, b_ref, out_ref):
    out_ref[...] = a_ref[...] + b_ref[...]


def joined(a, b):
    return small(join_kernel, [(a.shape[0] + b.shape[0],) + a.shape[1:]], a, b)


def added(a, b):
    return small(add_kernel, [a.shape], a, b)


def on_device(record, test_matrix):
    rows, _ = record.shape
    lags, _, width = test_matrix.shape
    n_time = lax.axis_size("tm")
    n_chan = lax.axis_size("chan")
    here = lax.axis_index("tm")
    mine = lax.axis_index("chan")
    half = n_time // 2
    mids = n_time // 4
    per = lags // n_time
    rim = lags
    place = jnp.stack(
        [mine, here, mine % 2, mine // 2, here % 2, here // half, (here % half) // 2]
    ).astype(jnp.int32)

    def to(block, target, axis="tm"):
        count = lax.axis_size(axis)
        route = [(i, target(i)) for i in range(count) if 0 <= target(i) < count]
        return lax.ppermute(block, axis, route)

    def to_both(block, target):
        route = []
        for t in range(n_time):
            for c in range(n_chan):
                a, b = target(t, c)
                if 0 <= a < n_time:
                    route.append((t * n_chan + c, a * n_chan + b))
        return lax.ppermute(block, ("tm", "chan"), route)

    def even(c):
        return c % 2 == 0

    def beside(t):
        return t ^ 1

    def across(t):
        return (t + half) % n_time

    cut = [0, rows // 2, 3 * rows // 4, rows]
    parts = cut_up(record, [b - a for a, b in zip(cut, cut[1:])])
    beside_record = to(record, beside)
    across_parts = [to(part, across) for part in parts]
    both_parts = [to(part, beside) for part in across_parts]

    keep, give = sketch(place, record, test_matrix, n_chan)
    share = keep.shape[1]
    got = to(give, lambda i: i ^ 1, "chan")
    own, passed = small(add_pair_kernel, [(1, share, width)] * 2, keep, got)
    own = added(own, to(passed, lambda i: i ^ 2, "chan"))

    own = joined(own, to_both(own, lambda t, c: (across(t), c)))
    got = to_both(own, lambda t, c: (t, c ^ 2) if even(c) else (beside(t), c))
    own = joined(own, got)
    got = to_both(own, lambda t, c: (beside(t), c) if even(c) else (t, c ^ 2))
    own = joined(own, got)
    edge = small(edges_kernel, [(own.shape[0] // 2, rim, width)], place, own, smem=1)
    got = to(own, lambda i: i ^ 1, "chan")

    def neighbour(t, step):
        middle = (t % half) // 2
        return t - 2 * middle + 2 * ((middle + step) % mids)

    edge = to_both(edge, lambda t, c: (neighbour(t, -1 if even(c) else 1), c))
    edge_got = to(edge, lambda i: i ^ 1, "chan")
    gram = gram_of(place, own, rim)
    gram_got = to(gram, lambda i: i ^ 1, "chan")
    sketches = assemble(place, own, got, edge, edge_got, n_chan, mids)
    gram = small(functools.partial(edge_gram_kernel, rim), [gram.shape], sketches, gram, gram_got)
    other = jnp.zeros_like(gram)
    distance = 2
    while distance < half:
        if distance > 2:
            gram = added(gram, other)
        other = to(gram, lambda i: i ^ distance)
        distance *= 2

    early = turn([record, beside_record, *across_parts[:2], both_parts[0]])
    late = turn([across_parts[2], *both_parts[1:]])
    turned = [early[0], early[2], early[3], late[0], early[1], early[4], late[1], late[2]]
    places = [(0, 0, rim)] + [(1, a, rim) for a in cut[:-1]] + [(2, 0, rim)] + [(3, a, rim) for a in cut[:-1]]

    middle = (here % half) // 2
    outer = here - 2 * middle

    def owner_lag(step):
        return (outer + 2 * ((middle + step) % mids)) * per

    chunks = max(per // 2, 1)
    size = per // chunks
    received = []
    for s in range(1, mids):
        def route(i):
            return neighbour(i, s)

        for n in range(chunks):
            part = lagged(owner_lag(s) + n * size, turned, places, sketches, size)
            received.append(to(part, route))
    kept = lagged(owner_lag(0), turned, places, sketches, per)
    inverse = factor(gram, other)

    basis = small(
        functools.partial(basis_kernel, float(rows * n_time) ** 0.5),
        [(rows, width)],
        inverse,
        sketches,
    )
    totals = []
    for n in range(chunks):
        total = received[n]
        for more in received[n + chunks :: chunks]:
            total = added(total, more)
        totals.append(total)
    coeffs = None
    for first, count in ((0, chunks - 1), (chunks - 1, 1)):
        if count:
            coeffs = finish(inverse, kept, totals[first : first + count], first, coeffs)
    return basis, coeffs


def solution(mesh):
    return jax.shard_map(
        on_device,
        mesh=mesh,
        in_specs=(P("tm", "chan"), P(None, "chan", None)),
        out_specs=(P("tm", None), P("tm", "chan", None)),
        check_vma=False,
    )
```
